32 devices in a mesh: seq: 8 (over z, y), tp: 4 (over x, core).
Axes of the slice: x: 2, y: 2, z: 4, core: 2. Of those that a mesh axis runs over, the one named last changes fastest.
Arguments:
- queries: bfloat16 [1024, 4096], P('seq', 'tp'), may hold values from -128 to 128
- keys: bfloat16 [1024, 4096], P('seq', 'tp'), may hold values from -6 to 6
- values: bfloat16 [1024, 4096], P('seq', 'tp'), may hold values from -18 to 18
- residual_in: bfloat16 [1024, 4096], P('seq', 'tp'), may hold values from -6 to 6
- norm_gain: float32 [4096], replicated, may hold values from 0.1 to 1.9
- routing: int32 [8, 1], replicated, may hold values from 0 to 3; in each aligned block of 8 rows (0 to 7, 8 to 15, ...) at most 4 rows name the same one
- gate_weight: bfloat16 [8, 4096, 512], P('seq', None, 'tp'), may hold values from -0.09375 to 0.09375
- up_weight: bfloat16 [8, 4096, 512], P('seq', None, 'tp'), may hold values from -0.09375 to 0.09375
- down_weight: bfloat16 [8, 512, 4096], P('seq', None, 'tp'), may hold values from -0.1875 to 0.1875
Outputs:
- mixed: bfloat16 [1024, 4096], P('seq', 'tp')
The draws below stay inside these ranges and needn't reach their ends.
Inputs may be any that keep to these rules, and one draw needn't show every extreme that they name: `routing`: every expert is named by some block; no expert by more than 4 blocks, and one by exactly 4.
All inputs are finite; a program needn't handle non-finite values.
Results may differ from the reference program's by a relative error of at most 0.006.
Values may be sent and summed in bfloat16 or wider, within the bound.
A program may use at most 64 MiB of HBM per device.

```python
import math
import jax
import jax.numpy as jnp
import numpy as np
from jax import lax

HEADS = 32
HEAD_DIM = 128
FF = 1024
BLOCK = 128
WINDOW = 512
D = 4096
TOKENS = 1024
NBLOCKS = 8
EXPERTS = 4
MOST = 4


def raw_keys(key):
    return jnp.clip(jax.random.normal(jax.random.fold_in(key, 11), (TOKENS, D), jnp.float32), -6.0, 6.0)


def draw_keys(key, part):
    base_keys = raw_keys(key)
    return base_keys.astype(jnp.bfloat16)


def draw_queries(key, part):
    drawn = jnp.clip(jax.random.normal(jax.random.fold_in(key, 12), (TOKENS, D), jnp.float32), -6.0, 6.0)
    return drawn.astype(jnp.bfloat16)


def shard_levels(own_key, dims, cuts, least, largest):
    level = 1.0
    for axis_at, blocks in cuts:
        heights = jax.random.uniform(jax.random.fold_in(jax.random.fold_in(own_key, 6), axis_at), (blocks,), jnp.float32, least / len(cuts), largest / len(cuts))
        level = level * jnp.repeat(jnp.exp(heights), dims[axis_at] // blocks).reshape((-1,) + (1,) * (len(dims) - 1 - axis_at))
    return level


def assign_block(stream_key, own, number, rows, count, top, bound, slope):
    sequence = jax.random.permutation(stream_key, count)
    packed, common = load_shares(count, rows * top, bound, slope, True), load_shares(count, rows * top, bound, slope, False)
    places = jnp.arange(count)

    def named(tallies, rotation):
        used = int((tallies > 0).sum())
        fixed = max(1, used // 4)
        moved = fixed + (places - fixed + rotation * (used - fixed)) % max(1, count - fixed)
        return jnp.zeros((count,), jnp.int32).at[sequence[jnp.where(places < fixed, places, moved)]].set(jnp.asarray(tallies, jnp.int32))

    tallies = jnp.where(number % 4 == 0, named(packed, number // 4), named(common, number - number // 4 - 1))
    mixed = jax.random.permutation(jax.random.fold_in(own, 3), count)
    source_of, receiver = mixed[0:count // 2 * 2:2], mixed[1:count // 2 * 2:2]
    margin = jnp.minimum(tallies[source_of] - 1, bound - tallies[receiver]) // 2
    margin = jnp.where((source_of == sequence[0]) | (receiver == sequence[0]) | (tallies[receiver] == 0), 0, jnp.maximum(margin, 0))
    moved = jax.random.randint(jax.random.fold_in(own, 4), (count // 2,), 0, 1 << 20) % (margin + 1)
    tallies = tallies.at[source_of].add(-moved).at[receiver].add(moved)
    labels = jnp.searchsorted(jnp.cumsum(tallies), jnp.arange(rows * top), side="right").astype(jnp.int32)
    listing = labels.reshape(top, rows).T
    listing = listing[jax.random.permutation(jax.random.fold_in(own, 1), rows)]
    rotation = jax.random.randint(jax.random.fold_in(own, 2), (rows, 1), 0, top)
    return jnp.take_along_axis(listing, (jnp.arange(top)[None, :] + rotation) % top, axis=1)


def load_shares(number_of, total, limit, lean, full):
    portions = [(1 << 20) // math.isqrt(grade ** lean) + 1 for grade in range(1, number_of + 1)]
    largest = limit if full else min(limit, max(-(-total // number_of), total * portions[0] // sum(portions)))
    least = 1 if total - largest >= number_of - 1 else 0
    holding, spare = [largest] + [least] * (number_of - 1), total - largest - least * (number_of - 1)
    while spare > 0:
        movable = [i for i in range(1, number_of) if holding[i] < largest] or [i for i in range(1, number_of) if holding[i] < limit]
        whole, left = sum([portions[i] for i in movable]), spare
        for i in movable:
            more = min(limit - holding[i], max(1, left * portions[i] // whole), spare)
            holding[i] = holding[i] + more
            spare = spare - more
    return np.array(holding)


def scatter_about(key, shape, deviation, most, shards=(), kind=jnp.bfloat16):
    factor_of = shard_levels(key, shape, shards, -0.22, 0.18) if shards else 1.0
    entries = jax.random.normal(key, shape, jnp.float32) * deviation * factor_of
    return jnp.minimum(jnp.maximum(entries, -most), most).astype(kind)


def setup_inputs(seed: int = 0) -> dict:
    arg_keys = jax.random.split(jax.random.key(seed), 10)
    queries = draw_queries(jax.random.fold_in(arg_keys[9], 71), 0)
    keys = draw_keys(jax.random.fold_in(arg_keys[9], 71), 0)
    values = scatter_about(arg_keys[2], (TOKENS, D), 3.0, 18.0, ((0, 8), (1, 4)))
    residual_in = scatter_about(arg_keys[3], (TOKENS, D), 1.0, 6.0, ((0, 8), (1, 4)))
    norm_gain = jnp.clip(1.0 + 0.18 * jax.random.normal(arg_keys[4], (D,), jnp.float32), 0.1, 1.9)
    routing_keys = jax.random.split(jax.random.fold_in(arg_keys[5], 1), NBLOCKS // NBLOCKS)
    routing_turns = jax.random.permutation(jax.random.fold_in(arg_keys[5], 3), NBLOCKS // NBLOCKS)
    routing = jax.vmap(lambda own, number: assign_block(jax.random.fold_in(arg_keys[5], 2), own, number, NBLOCKS, EXPERTS, 1, MOST, 2))(routing_keys, routing_turns).reshape((NBLOCKS, 1))
    gate_weight = scatter_about(arg_keys[6], (2 * EXPERTS, D, FF // 2), D ** -0.5, 0.09375, ((0, 8), (2, 4)))
    up_weight = scatter_about(arg_keys[7], (2 * EXPERTS, D, FF // 2), D ** -0.5, 0.09375, ((0, 8), (2, 4)))
    down_weight = scatter_about(arg_keys[8], (2 * EXPERTS, FF // 2, D), FF ** -0.5, 0.1875, ((0, 8), (2, 4)))
    return dict(queries=queries, keys=keys, values=values, residual_in=residual_in, norm_gain=norm_gain, routing=routing, gate_weight=gate_weight, up_weight=up_weight, down_weight=down_weight)


epsilon = 1e-05
masked_score = -1e+30

def attend_block(block_index, query_heads, key_padded, value_padded):
    begin_row = block_index * BLOCK
    query_block = lax.dynamic_slice_in_dim(query_heads, begin_row, BLOCK, 0).astype(jnp.float32)
    key_block = lax.dynamic_slice_in_dim(key_padded, begin_row, WINDOW + BLOCK, 0).astype(jnp.float32)
    value_block = lax.dynamic_slice_in_dim(value_padded, begin_row, WINDOW + BLOCK, 0).astype(jnp.float32)
    query_pos = begin_row + jnp.arange(BLOCK, dtype=jnp.int32)
    key_pos = begin_row - WINDOW + jnp.arange(WINDOW + BLOCK, dtype=jnp.int32)
    visible = (key_pos[None, :] >= 0) & (key_pos[None, :] <= query_pos[:, None]) & (key_pos[None, :] > query_pos[:, None] - WINDOW)
    scores = jnp.einsum('qhd,khd->hqk', query_block, key_block) * (1.0 / math.sqrt(HEAD_DIM))
    scores = jnp.where(visible[None], scores, masked_score)
    top_score = lax.optimization_barrier(jnp.max(scores, axis=2, keepdims=True))
    expo = jnp.exp(scores - top_score)
    weights_soft = (expo / lax.optimization_barrier(jnp.sum(expo, axis=2, keepdims=True))).astype(jnp.bfloat16)
    attended = jnp.einsum('hqk,khd->qhd', weights_soft.astype(jnp.float32), value_block)
    return attended.reshape(BLOCK, D)

def expert_block(stream_block, expert, norm_gain, gate_weight, up_weight, down_weight):
    stream_f32 = stream_block.astype(jnp.float32)
    mean_square = lax.optimization_barrier(jnp.mean(stream_f32 * stream_f32, axis=1, keepdims=True))
    normed = (stream_f32 * lax.rsqrt(mean_square + epsilon) * norm_gain).astype(jnp.bfloat16)
    summed = stream_f32
    for half_index in range(2):
        weight_row = (2 * expert + half_index).astype(jnp.int32)
        gate_rows = lax.dynamic_index_in_dim(gate_weight, weight_row, 0, keepdims=False)
        up_rows = lax.dynamic_index_in_dim(up_weight, weight_row, 0, keepdims=False)
        down_rows = lax.dynamic_index_in_dim(down_weight, weight_row, 0, keepdims=False)
        gate_val = jnp.dot(normed, gate_rows, preferred_element_type=jnp.float32)
        up_val = jnp.dot(normed, up_rows, preferred_element_type=jnp.float32)
        hidden = (jax.nn.silu(gate_val) * up_val).astype(jnp.bfloat16)
        branch = jnp.dot(hidden, down_rows, preferred_element_type=jnp.float32).astype(jnp.bfloat16)
        summed = summed + branch.astype(jnp.float32)
    return summed.astype(jnp.bfloat16)

def reference(queries, keys, values, residual_in, norm_gain, routing, gate_weight, up_weight, down_weight):
    query_heads = queries.reshape(TOKENS, HEADS, HEAD_DIM)
    zero_rows = jnp.zeros((WINDOW, D), keys.dtype)
    key_padded = jnp.concatenate([zero_rows, keys], axis=0).reshape(WINDOW + TOKENS, HEADS, HEAD_DIM)
    value_padded = jnp.concatenate([zero_rows, values], axis=0).reshape(WINDOW + TOKENS, HEADS, HEAD_DIM)
    attended = lax.map(lambda index: attend_block(index, query_heads, key_padded, value_padded), jnp.arange(NBLOCKS, dtype=jnp.int32))
    stream = (residual_in.reshape(NBLOCKS, BLOCK, D).astype(jnp.float32) + attended).astype(jnp.bfloat16)
    mixed = lax.map(lambda pair: expert_block(pair[0], pair[1], norm_gain, gate_weight, up_weight, down_weight), (stream, routing[:, 0]))
    return mixed.reshape(TOKENS, D)
```

```python
import math

import jax
import jax.numpy as jnp
from jax import lax
from jax.experimental import pallas as pl
from jax.experimental.pallas import tpu as pltpu
from jax.sharding import PartitionSpec as P

HEAD_DIM = 128
BLOCK = 128
WINDOW = 512


epsilon = 1e-05
masked_score = -1e30


def shifted(block, axis, distance):
    devices = range(lax.axis_size(axis))
    route = [(i - distance, i) for i in devices if i - distance in devices]
    return lax.ppermute(block, axis, route)


def local_general(
    queries, keys, values, residual_in, norm_gain, routing, gate_weight, up_weight, down_weight
):
    seq_count = lax.axis_size("seq")
    seq_place = lax.axis_index("seq")
    tok_rows = queries.shape[0]
    feat_width = queries.shape[1]
    head_count = feat_width // HEAD_DIM
    prior_count = (WINDOW - 1) // tok_rows + 1
    earlier_keys = []
    earlier_values = []
    for distance in range(1, prior_count + 1):
        moved_keys, moved_values = shifted((keys, values), "seq", distance)
        earlier_keys.insert(0, moved_keys)
        earlier_values.insert(0, moved_values)
    key_all = jnp.concatenate(earlier_keys + [keys], axis=0).reshape(-1, head_count, HEAD_DIM)
    value_all = jnp.concatenate(earlier_values + [values], axis=0).reshape(-1, head_count, HEAD_DIM)
    query_heads = queries.reshape(tok_rows, head_count, HEAD_DIM)
    query_pos = seq_place * tok_rows + jnp.arange(tok_rows, dtype=jnp.int32)
    key_pos = (
        seq_place * tok_rows
        - prior_count * tok_rows
        + jnp.arange((prior_count + 1) * tok_rows, dtype=jnp.int32)
    )
    visible = (
        (key_pos[None, :] >= 0)
        & (key_pos[None, :] <= query_pos[:, None])
        & (key_pos[None, :] > query_pos[:, None] - WINDOW)
    )
    scores = jnp.einsum(
        "qhd,khd->hqk", query_heads, key_all, preferred_element_type=jnp.float32
    ) * (1.0 / math.sqrt(HEAD_DIM))
    scores = jnp.where(visible[None], scores, masked_score)
    top_score = jnp.max(scores, axis=2, keepdims=True)
    expo = jnp.exp(scores - top_score)
    weights_soft = (expo / jnp.sum(expo, axis=2, keepdims=True)).astype(jnp.bfloat16)
    attended = jnp.einsum(
        "hqk,khd->qhd", weights_soft, value_all, preferred_element_type=jnp.float32
    ).reshape(tok_rows, feat_width)
    stream = (residual_in.astype(jnp.float32) + attended).astype(jnp.bfloat16)
    send_width = stream.shape[1]
    blocks_dev = tok_rows // BLOCK
    piece_rows = BLOCK // seq_count
    spread_in = stream.reshape(blocks_dev, seq_count, piece_rows, send_width)
    spread_out = lax.all_to_all(spread_in, "seq", split_axis=1, concat_axis=0, tiled=True)
    block_count = blocks_dev * seq_count
    spread_rows = spread_out.reshape(block_count, piece_rows, send_width)
    expert_ids = routing[:, 0]
    expert_count = seq_count // 2
    most_blocks = min(2 * block_count // expert_count, block_count - expert_count + 1)
    order_index = jnp.arange(block_count, dtype=jnp.int32)
    same_expert = expert_ids[None, :] == expert_ids[:, None]
    rank_of = jnp.sum(same_expert & (order_index[None, :] < order_index[:, None]), axis=1)
    expert_range = jnp.arange(expert_count, dtype=jnp.int32)
    slot_range = jnp.arange(most_blocks, dtype=jnp.int32)
    selector = (
        (expert_ids[None, None, :] == expert_range[:, None, None])
        & (rank_of[None, None, :] == slot_range[None, :, None])
    ).astype(jnp.bfloat16)
    picked = jnp.einsum(
        "erb,bqf->erqf", selector, spread_rows, preferred_element_type=jnp.float32
    ).astype(jnp.bfloat16)
    outgoing = jnp.broadcast_to(
        picked[:, None], (expert_count, 2, most_blocks, piece_rows, send_width)
    )
    outgoing = outgoing.reshape(seq_count, most_blocks, piece_rows, send_width)
    features_full = lax.all_gather(
        lax.all_to_all(outgoing, "seq", split_axis=0, concat_axis=0, tiled=True),
        "tp",
        axis=3,
        tiled=True,
    )
    source_count = features_full.shape[0]
    slot_count = features_full.shape[1]
    stream_f32 = features_full.astype(jnp.float32)
    mean_square = jnp.mean(stream_f32 * stream_f32, axis=3, keepdims=True)
    normed = (stream_f32 * lax.rsqrt(mean_square + epsilon) * norm_gain).astype(jnp.bfloat16)
    normed = normed.reshape(-1, normed.shape[3])
    gate_val = jnp.dot(normed, gate_weight[0], preferred_element_type=jnp.float32)
    up_val = jnp.dot(normed, up_weight[0], preferred_element_type=jnp.float32)
    hidden = (jax.nn.silu(gate_val) * up_val).astype(jnp.bfloat16)
    hidden_half = lax.all_gather(hidden, "tp", axis=1, tiled=True)
    partial_value = jnp.dot(hidden_half, down_weight[0], preferred_element_type=jnp.float32).astype(
        jnp.bfloat16
    )
    partial_value = partial_value.reshape(source_count, slot_count, piece_rows, feat_width)
    returned = lax.all_to_all(partial_value, "seq", split_axis=0, concat_axis=0, tiled=True)
    returned = returned.reshape(expert_count, 2, most_blocks, piece_rows * feat_width)
    combined = jnp.einsum("erb,epry->pby", selector, returned, preferred_element_type=jnp.float32)
    residual_rows = spread_rows
    residual_rows = residual_rows.reshape(block_count, piece_rows * feat_width).astype(jnp.float32)
    finished = (residual_rows + combined[0] + combined[1]).astype(jnp.bfloat16)
    finished = finished.reshape(seq_count, blocks_dev, piece_rows, feat_width)
    restored = lax.all_to_all(finished, "seq", split_axis=0, concat_axis=2, tiled=True)
    return restored.reshape(tok_rows, feat_width)


BF16 = jnp.bfloat16
F32 = jnp.float32


def remote(src, dst, send_sem, recv_sem, device):
    return pltpu.make_async_remote_copy(
        src_ref=src,
        dst_ref=dst,
        send_sem=send_sem,
        recv_sem=recv_sem,
        device_id=device,
        device_id_type=pl.DeviceIdType.MESH,
    )


def layer_kernel(
    planes,
    most,
    routing_ref,
    q_ref,
    k_ref,
    v_ref,
    r_ref,
    gain_ref,
    gate_ref,
    up_ref,
    down_ref,
    out_ref,
    q_buf,
    r_buf,
    kv_buf,
    line_buf,
    x_buf,
    w_buf,
    acc_buf,
    square_buf,
    hid_buf,
    down_buf,
    mix_buf,
    up_out,
    up_in,
    dn_out,
    dn_in,
    fin_buf,
    pair_s,
    pair_r,
    local_s,
    kvline_s,
    kvline_r,
    line_s,
    line_r,
    feat_s,
    feat_r,
    hid_s,
    hid_r,
    ret_s,
    ret_r,
    last_s,
    last_r,
):
    rows = q_ref.shape[0]
    half = q_ref.shape[1] // 2
    heads = half // HEAD_DIM
    blocks = 2 * planes
    me = lax.axis_index("seq")
    t = lax.axis_index("tp")
    z = me // 2
    y = me % 2
    yo = 1 - y
    mate = 2 * z + yo
    tc = t + 1 - 2 * (t % 2)
    tx = t + 2 - 4 * (t // 2)
    txc = tx + 1 - 2 * (tx % 2)
    dev_y, dev_c, dev_x = (mate, t), (me, tc), (me, tx)
    dev_up, dev_dn = (me + 2, t), (me - 2, t)
    has_up, has_dn = z < planes - 1, z > 0
    unsent = []

    barrier = pltpu.get_barrier_semaphore()

    def greet(device):
        pl.semaphore_signal(
            barrier, inc=1, device_id=device, device_id_type=pl.DeviceIdType.MESH
        )

    for device in (dev_y, dev_c, dev_x):
        greet(device)
    pl.when(has_up)(lambda: greet(dev_up))
    pl.when(has_dn)(lambda: greet(dev_dn))

    def cols(which, h):
        return pl.ds(pl.multiple_of(which * half + h * HEAD_DIM, HEAD_DIM), HEAD_DIM)

    def wide(which):
        return pl.ds(pl.multiple_of(which * half, half), half)

    stay = []
    for h in range(heads):
        stay.append((k_ref.at[:, cols(y, h)], kv_buf.at[0, h, 0, y]))
        stay.append((v_ref.at[:, cols(y, h)], kv_buf.at[0, h, 1, y]))
    stay.append((q_ref.at[:, wide(y)], q_buf.at[y]))
    stay.append((r_ref.at[:, wide(y)], r_buf.at[y]))
    stay.append((gate_ref.at[0], w_buf.at[:, pl.ds(0, gate_ref.shape[2])]))
    stay.append((up_ref.at[0], w_buf.at[:, pl.ds(gate_ref.shape[2], gate_ref.shape[2])]))
    stay.append((down_ref.at[0, :, wide(y)], down_buf.at[y]))
    stay = [pltpu.make_async_copy(a, b, local_s.at[i]) for i, (a, b) in enumerate(stay)]
    for copy in stay:
        copy.start()

    expert = [routing_ref[b, 0] for b in range(blocks)]
    slot = []
    for b in range(blocks):
        count = jnp.int32(0)
        for j in range(b):
            count = count + jnp.where(expert[j] == expert[b], 1, 0)
        slot.append(jnp.minimum(count, most - 1))
    chosen = []
    for r in range(most):
        index = jnp.int32(0)
        for b in range(blocks):
            index = jnp.where((expert[b] == z) & (slot[b] == r), b, index)
        chosen.append(index)

    for dist in (1, 2):

        @pl.when(z < dist)
        def _():
            kv_buf[dist] = jnp.zeros(kv_buf.shape[1:], kv_buf.dtype)

    pl.semaphore_wait(
        barrier, 3 + jnp.where(has_up, 1, 0) + jnp.where(has_dn, 1, 0)
    )

    def pair_copy(i, src, dst):
        return remote(src, dst, pair_s.at[i], pair_r.at[i], dev_y)

    swap, landed = [], []
    for h in range(heads):
        for n, ref in enumerate((k_ref, v_ref)):
            i = len(swap)
            swap.append(pair_copy(i, ref.at[:, cols(yo, h)], kv_buf.at[0, h, n, y]))
            landed.append(pair_copy(i, kv_buf.at[0, h, n, yo], kv_buf.at[0, h, n, yo]))
    for ref, buf in ((q_ref, q_buf), (r_ref, r_buf)):
        i = len(swap)
        swap.append(pair_copy(i, ref.at[:, wide(yo)], buf.at[y]))
        landed.append(pair_copy(i, buf.at[yo], buf.at[yo]))
    i = len(swap)
    swap.append(pair_copy(i, down_ref.at[0, :, wide(yo)], down_buf.at[y + 2]))
    landed.append(pair_copy(i, down_buf.at[yo + 2], down_buf.at[yo + 2]))
    for copy in swap:
        copy.start()
        unsent.append((None, copy))

    def kv_copy(dist, h):
        return remote(
            kv_buf.at[dist, h],
            kv_buf.at[dist + 1, h],
            kvline_s.at[dist, h],
            kvline_r.at[dist, h],
            dev_up,
        )

    def kv_own(h):
        for i in (2 * h, 2 * h + 1):
            stay[i].wait()
            landed[i].wait_recv()
        pl.when(has_up)(lambda: kv_copy(0, h).start())
        unsent.append((has_up, kv_copy(0, h)))

    def kv_relay(h):
        pl.when(has_dn)(lambda: kv_copy(0, h).wait_recv())
        pl.when(has_dn & has_up)(lambda: kv_copy(1, h).start())
        unsent.append((has_dn & has_up, kv_copy(1, h)))

    def line_copy(way, plane, h):
        return remote(
            line_buf.at[plane, h],
            line_buf.at[plane, h],
            line_s.at[way, plane, h],
            line_r.at[way, plane, h],
            dev_up if way == 0 else dev_dn,
        )

    query_at = lax.broadcasted_iota(jnp.int32, (2 * rows, 2 * rows), 0)
    key_at = lax.broadcasted_iota(jnp.int32, (2 * rows, 2 * rows), 1)

    def attend(h):
        pl.when(z > 1)(lambda: kv_copy(1, h).wait_recv())
        at = pl.ds(h * HEAD_DIM, HEAD_DIM)
        query = q_buf[:, :, at].reshape(2 * rows, HEAD_DIM)
        parts = []
        for dist in range(3):
            key = kv_buf[dist, h, 0].reshape(2 * rows, HEAD_DIM)
            score = lax.dot_general(
                query, key, (((1,), (1,)), ((), ())), preferred_element_type=F32
            ) * (1.0 / math.sqrt(HEAD_DIM))
            gap = query_at - key_at + 2 * rows * dist
            seen = (gap >= 0) & (gap < WINDOW) & (jnp.full(gap.shape, z, jnp.int32) >= dist)
            parts.append(jnp.where(seen, score, masked_score))
        top = jnp.max(parts[0], axis=1, keepdims=True)
        for part in parts[1:]:
            top = jnp.maximum(top, jnp.max(part, axis=1, keepdims=True))
        parts = [jnp.exp(part - top) for part in parts]
        total = sum(jnp.sum(part, axis=1, keepdims=True) for part in parts)
        result = r_buf[:, :, at].reshape(2 * rows, HEAD_DIM).astype(F32)
        attended = None
        for dist in range(3):
            value = kv_buf[dist, h, 1].reshape(2 * rows, HEAD_DIM)
            term = jnp.dot((parts[dist] / total).astype(BF16), value, preferred_element_type=F32)
            attended = term if attended is None else attended + term
        stream = (result + attended).astype(BF16)
        line_buf[z, h] = stream.reshape(2, rows, HEAD_DIM)
        pl.when(has_up)(lambda: line_copy(0, z, h).start())
        pl.when(has_dn)(lambda: line_copy(1, z, h).start())
        unsent.append((has_up, line_copy(0, z, h)))
        unsent.append((has_dn, line_copy(1, z, h)))

    for h in range(heads):
        kv_own(h)
    kv_relay(0)
    for i in (2 * heads, 2 * heads + 1):
        stay[i].wait()
        landed[i].wait_recv()
    for h in range(heads):
        if h + 1 < heads:
            kv_relay(h + 1)
        attend(h)

    for step in range(1, planes):
        below, above = z - step, z + step
        for h in range(heads):

            @pl.when(below >= 0)
            def _():
                line_copy(0, below, h).wait_recv()
                pl.when(has_up)(lambda: line_copy(0, below, h).start())

            unsent.append(((below >= 0) & has_up, line_copy(0, below, h)))

            @pl.when(above < planes)
            def _():
                line_copy(1, above, h).wait_recv()
                pl.when(has_dn)(lambda: line_copy(1, above, h).start())

            unsent.append(((above < planes) & has_dn, line_copy(1, above, h)))

    for r in range(most):
        for h in range(heads):
            x_buf[y, t, pl.ds(r * rows, rows), pl.ds(h * HEAD_DIM, HEAD_DIM)] = line_buf[
                chosen[r] // 2, h, chosen[r] % 2
            ]

    def gather(buf, sends, recvs, consume):
        middle = buf.shape[2] // 2
        low, high = pl.ds(0, middle), pl.ds(middle, middle)

        def piece(i, at, device):
            ref = buf.at[at[0], at[1]] if at[2] is None else buf.at[at[0], at[1], at[2]]
            return remote(ref, ref, sends.at[i], recvs.at[i], device)

        def send(i, at, device):
            piece(i, at, device).start()
            unsent.append((None, piece(i, at, device)))

        def take(i, at):
            piece(i, at, dev_c).wait_recv()

        send(0, (y, t, low), dev_x)
        send(1, (y, t, high), dev_y)
        send(2, (y, t, high), dev_x)
        send(3, (y, t, low), dev_y)
        send(4, (y, t, None), dev_c)
        consume(y, t)
        take(4, (y, tc, None))
        consume(y, tc)
        take(0, (y, tx, low))
        send(5, (y, tx, low), dev_y)
        send(7, (y, tx, low), dev_c)
        take(1, (yo, t, high))
        send(6, (yo, t, high), dev_x)
        send(8, (yo, t, high), dev_c)
        take(2, (y, tx, high))
        send(9, (y, tx, high), dev_c)
        take(3, (yo, t, low))
        send(10, (yo, t, low), dev_c)
        consume(y, tx)
        consume(yo, t)
        take(7, (y, txc, low))
        take(9, (y, txc, high))
        consume(y, txc)
        take(8, (yo, tc, high))
        take(10, (yo, tc, low))
        consume(yo, tc)
        take(5, (yo, tx, low))
        send(11, (yo, tx, low), dev_c)
        take(6, (yo, tx, high))
        send(12, (yo, tx, high), dev_c)
        consume(yo, tx)
        take(11, (yo, txc, low))
        take(12, (yo, txc, high))
        consume(yo, txc)

    acc_buf[...] = jnp.zeros_like(acc_buf)
    square_buf[...] = jnp.zeros_like(square_buf)
    for copy in stay[2 * heads + 2 :]:
        copy.wait()

    def expert_part(py, pt):
        start = pl.multiple_of((2 * pt + py) * half, half)
        x = x_buf[py, pt].astype(F32)
        square_buf[...] += jnp.sum(x * x, axis=1, keepdims=True)
        scaled = (x * gain_ref[:, pl.ds(start, half)]).astype(BF16)
        acc_buf[...] += jnp.dot(scaled, w_buf[pl.ds(start, half), :], preferred_element_type=F32)

    gather(x_buf, feat_s, feat_r, expert_part)
    units = gate_ref.shape[2]
    features = gain_ref.shape[1]
    scale = lax.rsqrt(square_buf[...] * (1.0 / features) + epsilon)
    gate_val = acc_buf[:, pl.ds(0, units)] * scale
    up_val = acc_buf[:, pl.ds(units, units)] * scale
    hid_buf[y, t] = (gate_val / (1.0 + jnp.exp(-gate_val)) * up_val).astype(BF16)
    gather(hid_buf, hid_s, hid_r, lambda py, pt: None)

    landed[2 * heads + 2].wait_recv()
    branches = []
    for h in range(2):
        hidden = jnp.concatenate([hid_buf[h, i] for i in range(hid_buf.shape[1])], axis=1)
        weight = down_buf[h + 2 * ((y + h) % 2)]
        branches.append(jnp.dot(hidden, weight, preferred_element_type=F32).astype(BF16))
    mixed = x_buf[y, t].astype(F32) + branches[0].astype(F32) + branches[1].astype(F32)
    mix_buf[...] = mixed.astype(BF16).reshape(mix_buf.shape)

    def ret_copy(way, d):
        if way == 0:
            return remote(up_out.at[d], up_in.at[d], ret_s.at[0, d], ret_r.at[0, d], dev_up)
        return remote(dn_out.at[d], dn_in.at[d], ret_s.at[1, d], ret_r.at[1, d], dev_dn)

    def own(b):
        return mix_buf[slot[b]]

    def pick(flag, a, b):
        mask = jnp.full(a.shape, flag.astype(jnp.int32), jnp.int32) > 0
        return jnp.where(mask, a.astype(F32), b.astype(F32)).astype(BF16)

    for step in range(planes - 1):
        for way, d in ((0, planes - 1 - step), (1, step)):
            passes = z < d if way == 0 else z > d
            first = z == 0 if way == 0 else z == planes - 1
            out, arrived = (up_out, up_in) if way == 0 else (dn_out, dn_in)

            @pl.when(passes & first)
            def _():
                for n in range(2):
                    out[d, n] = own(2 * d + n)

            @pl.when(passes & jnp.logical_not(first))
            def _():
                ret_copy(way, d).wait_recv()
                for n in range(2):
                    b = 2 * d + n
                    out[d, n] = pick(expert[b] == z, own(b), arrived[d, n])

            pl.when(passes)(lambda: ret_copy(way, d).start())
            unsent.append((passes, ret_copy(way, d)))

    last = remote(
        fin_buf.at[yo], out_ref.at[:, wide(y)], last_s.at[0], last_r.at[0], dev_y
    )
    for d in range(planes):

        @pl.when(z == d)
        def _():
            if d > 0:
                ret_copy(0, d).wait_recv()
            if d < planes - 1:
                ret_copy(1, d).wait_recv()
            for n in range(2):
                b = 2 * d + n
                value = own(b)
                if d > 0:
                    value = pick(expert[b] < z, up_in[d, n], value)
                if d < planes - 1:
                    value = pick(expert[b] > z, dn_in[d, n], value)
                fin_buf[n] = value

    last.start()
    out_ref[:, wide(y)] = fin_buf[y]
    remote(
        out_ref.at[:, wide(yo)], out_ref.at[:, wide(yo)], last_s.at[0], last_r.at[0], dev_y
    ).wait_recv()
    last.wait_send()
    for flag, copy in unsent:
        if flag is None:
            copy.wait_send()
        else:
            pl.when(flag)(lambda: copy.wait_send())


def local(
    queries, keys, values, residual_in, norm_gain, routing, gate_weight, up_weight, down_weight
):
    seq_count = lax.axis_size("seq")
    tp_count = lax.axis_size("tp")
    rows, width = queries.shape
    units = gate_weight.shape[2]
    planes = seq_count // 2
    fits = (
        tp_count == 4
        and seq_count % 2 == 0
        and 3 <= planes <= 8
        and rows == BLOCK
        and WINDOW == 4 * rows
        and units == 128
        and width % (2 * HEAD_DIM) == 0
    )
    if not fits:
        return local_general(
            queries,
            keys,
            values,
            residual_in,
            norm_gain,
            routing,
            gate_weight,
            up_weight,
            down_weight,
        )
    half = width // 2
    heads = half // HEAD_DIM
    most = min(2 * seq_count // planes, seq_count - planes + 1)
    features = norm_gain.shape[0]
    vmem = pl.BlockSpec(memory_space=pltpu.VMEM)
    anywhere = pl.BlockSpec(memory_space=pl.ANY)
    dma = pltpu.SemaphoreType.DMA
    return pl.pallas_call(
        lambda *refs: layer_kernel(planes, most, *refs),
        name="layer",
        out_shape=jax.ShapeDtypeStruct((rows, width), BF16),
        in_specs=[pl.BlockSpec(memory_space=pltpu.SMEM)]
        + [anywhere] * 4
        + [vmem]
        + [anywhere] * 3,
        out_specs=vmem,
        scratch_shapes=[
            pltpu.VMEM((2, rows, half), BF16),
            pltpu.VMEM((2, rows, half), BF16),
            pltpu.VMEM((3, heads, 2, 2, rows, HEAD_DIM), BF16),
            pltpu.VMEM((planes, heads, 2, rows, HEAD_DIM), BF16),
            pltpu.VMEM((2, tp_count, most * rows, half), BF16),
            pltpu.VMEM((features, 2 * units), BF16),
            pltpu.VMEM((most * rows, 2 * units), F32),
            pltpu.VMEM((most * rows, 1), F32),
            pltpu.VMEM((2, tp_count, most * rows, units), BF16),
            pltpu.VMEM((4, down_weight.shape[1], half), BF16),
            pltpu.VMEM((most, rows, half), BF16),
            pltpu.VMEM((planes, 2, rows, half), BF16),
            pltpu.VMEM((planes, 2, rows, half), BF16),
            pltpu.VMEM((planes, 2, rows, half), BF16),
            pltpu.VMEM((planes, 2, rows, half), BF16),
            pltpu.VMEM((2, rows, half), BF16),
            dma((2 * heads + 3,)),
            dma((2 * heads + 3,)),
            dma((2 * heads + 5,)),
            dma((2, heads)),
            dma((2, heads)),
            dma((2, planes, heads)),
            dma((2, planes, heads)),
            dma((13,)),
            dma((13,)),
            dma((13,)),
            dma((13,)),
            dma((2, planes)),
            dma((2, planes)),
            dma((1,)),
            dma((1,)),
        ],
        compiler_params=pltpu.CompilerParams(
            collective_id=0, has_side_effects=True, vmem_limit_bytes=48 * 1024 * 1024
        ),
    )(
        routing,
        queries,
        keys,
        values,
        residual_in,
        norm_gain.reshape(1, features),
        gate_weight,
        up_weight,
        down_weight,
    )


def solution(mesh):
    in_specs = (
        P("seq", "tp"),
        P("seq", "tp"),
        P("seq", "tp"),
        P("seq", "tp"),
        P(),
        P(),
        P("seq", None, "tp"),
        P("seq", None, "tp"),
        P("seq", None, "tp"),
    )
    out_specs = P("seq", "tp")
    return jax.shard_map(local, mesh=mesh, in_specs=in_specs, out_specs=out_specs, check_vma=False)
```

```python
import math

import jax
import jax.numpy as jnp
from jax import lax
from jax.experimental import pallas as pl
from jax.experimental.pallas import tpu as pltpu
from jax.sharding import PartitionSpec as P

HEAD_DIM = 128
BLOCK = 128
WINDOW = 512


epsilon = 1e-05
masked_score = -1e30


def shifted(block, axis, distance):
    devices = range(lax.axis_size(axis))
    route = [(i - distance, i) for i in devices if i - distance in devices]
    return lax.ppermute(block, axis, route)


def local_general(
    queries, keys, values, residual_in, norm_gain, routing, gate_weight, up_weight, down_weight
):
    seq_count = lax.axis_size("seq")
    seq_place = lax.axis_index("seq")
    tok_rows = queries.shape[0]
    feat_width = queries.shape[1]
    head_count = feat_width // HEAD_DIM
    prior_count = (WINDOW - 1) // tok_rows + 1
    earlier_keys = []
    earlier_values = []
    for distance in range(1, prior_count + 1):
        moved_keys, moved_values = shifted((keys, values), "seq", distance)
        earlier_keys.insert(0, moved_keys)
        earlier_values.insert(0, moved_values)
    key_all = jnp.concatenate(earlier_keys + [keys], axis=0).reshape(-1, head_count, HEAD_DIM)
    value_all = jnp.concatenate(earlier_values + [values], axis=0).reshape(-1, head_count, HEAD_DIM)
    query_heads = queries.reshape(tok_rows, head_count, HEAD_DIM)
    query_pos = seq_place * tok_rows + jnp.arange(tok_rows, dtype=jnp.int32)
    key_pos = (
        seq_place * tok_rows
        - prior_count * tok_rows
        + jnp.arange((prior_count + 1) * tok_rows, dtype=jnp.int32)
    )
    visible = (
        (key_pos[None, :] >= 0)
        & (key_pos[None, :] <= query_pos[:, None])
        & (key_pos[None, :] > query_pos[:, None] - WINDOW)
    )
    scores = jnp.einsum(
        "qhd,khd->hqk", query_heads, key_all, preferred_element_type=jnp.float32
    ) * (1.0 / math.sqrt(HEAD_DIM))
    scores = jnp.where(visible[None], scores, masked_score)
    top_score = jnp.max(scores, axis=2, keepdims=True)
    expo = jnp.exp(scores - top_score)
    weights_soft = (expo / jnp.sum(expo, axis=2, keepdims=True)).astype(jnp.bfloat16)
    attended = jnp.einsum(
        "hqk,khd->qhd", weights_soft, value_all, preferred_element_type=jnp.float32
    ).reshape(tok_rows, feat_width)
    stream = (residual_in.astype(jnp.float32) + attended).astype(jnp.bfloat16)
    send_width = stream.shape[1]
    blocks_dev = tok_rows // BLOCK
    piece_rows = BLOCK // seq_count
    spread_in = stream.reshape(blocks_dev, seq_count, piece_rows, send_width)
    spread_out = lax.all_to_all(spread_in, "seq", split_axis=1, concat_axis=0, tiled=True)
    block_count = blocks_dev * seq_count
    spread_rows = spread_out.reshape(block_count, piece_rows, send_width)
    expert_ids = routing[:, 0]
    expert_count = seq_count // 2
    most_blocks = min(2 * block_count // expert_count, block_count - expert_count + 1)
    order_index = jnp.arange(block_count, dtype=jnp.int32)
    same_expert = expert_ids[None, :] == expert_ids[:, None]
    rank_of = jnp.sum(same_expert & (order_index[None, :] < order_index[:, None]), axis=1)
    expert_range = jnp.arange(expert_count, dtype=jnp.int32)
    slot_range = jnp.arange(most_blocks, dtype=jnp.int32)
    selector = (
        (expert_ids[None, None, :] == expert_range[:, None, None])
        & (rank_of[None, None, :] == slot_range[None, :, None])
    ).astype(jnp.bfloat16)
    picked = jnp.einsum(
        "erb,bqf->erqf", selector, spread_rows, preferred_element_type=jnp.float32
    ).astype(jnp.bfloat16)
    outgoing = jnp.broadcast_to(
        picked[:, None], (expert_count, 2, most_blocks, piece_rows, send_width)
    )
    outgoing = outgoing.reshape(seq_count, most_blocks, piece_rows, send_width)
    features_full = lax.all_gather(
        lax.all_to_all(outgoing, "seq", split_axis=0, concat_axis=0, tiled=True),
        "tp",
        axis=3,
        tiled=True,
    )
    source_count = features_full.shape[0]
    slot_count = features_full.shape[1]
    stream_f32 = features_full.astype(jnp.float32)
    mean_square = jnp.mean(stream_f32 * stream_f32, axis=3, keepdims=True)
    normed = (stream_f32 * lax.rsqrt(mean_square + epsilon) * norm_gain).astype(jnp.bfloat16)
    normed = normed.reshape(-1, normed.shape[3])
    gate_val = jnp.dot(normed, gate_weight[0], preferred_element_type=jnp.float32)
    up_val = jnp.dot(normed, up_weight[0], preferred_element_type=jnp.float32)
    hidden = (jax.nn.silu(gate_val) * up_val).astype(jnp.bfloat16)
    hidden_half = lax.all_gather(hidden, "tp", axis=1, tiled=True)
    partial_value = jnp.dot(hidden_half, down_weight[0], preferred_element_type=jnp.float32).astype(
        jnp.bfloat16
    )
    partial_value = partial_value.reshape(source_count, slot_count, piece_rows, feat_width)
    returned = lax.all_to_all(partial_value, "seq", split_axis=0, concat_axis=0, tiled=True)
    returned = returned.reshape(expert_count, 2, most_blocks, piece_rows * feat_width)
    combined = jnp.einsum("erb,epry->pby", selector, returned, preferred_element_type=jnp.float32)
    residual_rows = spread_rows
    residual_rows = residual_rows.reshape(block_count, piece_rows * feat_width).astype(jnp.float32)
    finished = (residual_rows + combined[0] + combined[1]).astype(jnp.bfloat16)
    finished = finished.reshape(seq_count, blocks_dev, piece_rows, feat_width)
    restored = lax.all_to_all(finished, "seq", split_axis=0, concat_axis=2, tiled=True)
    return restored.reshape(tok_rows, feat_width)


BF16 = jnp.bfloat16
F32 = jnp.float32


def remote(src, dst, send_sem, recv_sem, device):
    return pltpu.make_async_remote_copy(
        src_ref=src,
        dst_ref=dst,
        send_sem=send_sem,
        recv_sem=recv_sem,
        device_id=device,
        device_id_type=pl.DeviceIdType.MESH,
    )


def layer_kernel(planes, most, arguments, out_ref, scratch):
    (
        routing_ref, q_ref, k_ref, v_ref, r_ref, gain_ref, gate_ref, up_ref, down_ref
    ) = arguments
    (
        q_buf,
        r_buf,
        kv_buf,
        line,
        end_out,
        end_in,
        x_buf,
        w_buf,
        acc_buf,
        square_buf,
        hid_buf,
        down_buf,
        mix,
        end_up,
        end_dn,
        up_out,
        up_in,
        dn_out,
        dn_in,
        fin_buf,
        pair_s,
        pair_r,
        local_s,
        kvline_s,
        kvline_r,
        line_s,
        line_r,
        end_s,
        end_r,
        feat_s,
        feat_r,
        hid_s,
        hid_r,
        ret_s,
        ret_r,
        edge_s,
        edge_r,
        last_s,
        last_r,
    ) = scratch
    rows = q_ref.shape[0]
    half = q_ref.shape[1] // 2
    heads = half // HEAD_DIM
    blocks = 2 * planes
    me = lax.axis_index("seq")
    t = lax.axis_index("tp")
    z = me // 2
    y = me % 2
    yo = 1 - y
    mate = 2 * z + yo
    tc = t + 1 - 2 * (t % 2)
    tx = t + 2 - 4 * (t // 2)
    txc = tx + 1 - 2 * (tx % 2)
    dev_y, dev_c, dev_x = (mate, t), (me, tc), (me, tx)
    dev_up, dev_dn = (me + 2, t), (me - 2, t)
    has_up, has_dn = z < planes - 1, z > 0
    unsent = []

    barrier = pltpu.get_barrier_semaphore()

    def greet(device):
        pl.semaphore_signal(
            barrier, inc=1, device_id=device, device_id_type=pl.DeviceIdType.MESH
        )

    for device in (dev_y, dev_c, dev_x):
        greet(device)
    pl.when(has_up)(lambda: greet(dev_up))
    pl.when(has_dn)(lambda: greet(dev_dn))

    def cols(which, h):
        return pl.ds(pl.multiple_of(which * half + h * HEAD_DIM, HEAD_DIM), HEAD_DIM)

    def wide(which):
        return pl.ds(pl.multiple_of(which * half, half), half)

    stay = []
    for h in range(heads):
        stay.append((k_ref.at[:, cols(y, h)], kv_buf.at[0, h, 0, y]))
        stay.append((v_ref.at[:, cols(y, h)], kv_buf.at[0, h, 1, y]))
    stay.append((q_ref.at[:, wide(y)], q_buf.at[y]))
    stay.append((r_ref.at[:, wide(y)], r_buf.at[y]))
    stay.append((gate_ref.at[0], w_buf.at[:, pl.ds(0, gate_ref.shape[2])]))
    stay.append((up_ref.at[0], w_buf.at[:, pl.ds(gate_ref.shape[2], gate_ref.shape[2])]))
    stay.append((down_ref.at[0, :, wide(y)], down_buf.at[y]))
    stay = [pltpu.make_async_copy(a, b, local_s.at[i]) for i, (a, b) in enumerate(stay)]
    for copy in stay:
        copy.start()

    expert = [routing_ref[b, 0] for b in range(blocks)]
    slot = []
    for b in range(blocks):
        count = jnp.int32(0)
        for j in range(b):
            count = count + jnp.where(expert[j] == expert[b], 1, 0)
        slot.append(jnp.minimum(count, most - 1))

    def listing(which):
        found = []
        for r in range(most):
            index = jnp.int32(0)
            for b in range(blocks):
                index = jnp.where((expert[b] == which) & (slot[b] == r), b, index)
            found.append(index)
        return found

    chosen = listing(z)
    at_edge = (z == 0) | (z == planes - 1)
    by_edge = (z == 1) | (z == planes - 2)
    chosen_edge = listing(jnp.where(z == 1, 0, planes - 1))
    dev_edge = (jnp.where(z == 1, me - 2, me + 2), t)
    line_up, line_dn = z < planes - 2, z > 1

    for dist in (1, 2):

        @pl.when(z < dist)
        def _():
            kv_buf[dist] = jnp.zeros(kv_buf.shape[1:], kv_buf.dtype)

    pl.semaphore_wait(
        barrier, 3 + jnp.where(has_up, 1, 0) + jnp.where(has_dn, 1, 0)
    )

    def pair_copy(i, src, dst):
        return remote(src, dst, pair_s.at[i], pair_r.at[i], dev_y)

    swap, landed = [], []
    for h in range(heads):
        for n, ref in enumerate((k_ref, v_ref)):
            i = len(swap)
            swap.append(pair_copy(i, ref.at[:, cols(yo, h)], kv_buf.at[0, h, n, y]))
            landed.append(pair_copy(i, kv_buf.at[0, h, n, yo], kv_buf.at[0, h, n, yo]))
    for ref, buf in ((q_ref, q_buf), (r_ref, r_buf)):
        i = len(swap)
        swap.append(pair_copy(i, ref.at[:, wide(yo)], buf.at[y]))
        landed.append(pair_copy(i, buf.at[yo], buf.at[yo]))
    i = len(swap)
    swap.append(pair_copy(i, down_ref.at[0, :, wide(yo)], down_buf.at[y + 2]))
    landed.append(pair_copy(i, down_buf.at[yo + 2], down_buf.at[yo + 2]))
    for copy in swap:
        copy.start()
        unsent.append((None, copy))

    def kv_copy(dist, h):
        return remote(
            kv_buf.at[dist, h],
            kv_buf.at[dist + 1, h],
            kvline_s.at[dist, h],
            kvline_r.at[dist, h],
            dev_up,
        )

    def kv_own(h):
        for i in (2 * h, 2 * h + 1):
            stay[i].wait()
            landed[i].wait_recv()
        pl.when(has_up)(lambda: kv_copy(0, h).start())
        unsent.append((has_up, kv_copy(0, h)))

    def kv_relay(h):
        pl.when(has_dn)(lambda: kv_copy(0, h).wait_recv())
        pl.when(has_dn & has_up)(lambda: kv_copy(1, h).start())
        unsent.append((has_dn & has_up, kv_copy(1, h)))

    def line_copy(way, plane, h):
        return remote(
            line[h].at[plane],
            line[h].at[plane],
            line_s.at[way, plane, h],
            line_r.at[way, plane, h],
            dev_up if way == 0 else dev_dn,
        )

    query_at = lax.broadcasted_iota(jnp.int32, (2 * rows, 2 * rows), 0)
    key_at = lax.broadcasted_iota(jnp.int32, (2 * rows, 2 * rows), 1)

    def attend(h):
        pl.when(z > 1)(lambda: kv_copy(1, h).wait_recv())
        at = pl.ds(h * HEAD_DIM, HEAD_DIM)
        query = q_buf[:, :, at].reshape(2 * rows, HEAD_DIM)
        parts = []
        for dist in range(3):
            key = kv_buf[dist, h, 0].reshape(2 * rows, HEAD_DIM)
            score = lax.dot_general(
                query, key, (((1,), (1,)), ((), ())), preferred_element_type=F32
            ) * (1.0 / math.sqrt(HEAD_DIM))
            gap = query_at - key_at + 2 * rows * dist
            seen = (gap >= 0) & (gap < WINDOW) & (jnp.full(gap.shape, z, jnp.int32) >= dist)
            parts.append(jnp.where(seen, score, masked_score))
        top = jnp.max(parts[0], axis=1, keepdims=True)
        for part in parts[1:]:
            top = jnp.maximum(top, jnp.max(part, axis=1, keepdims=True))
        parts = [jnp.exp(part - top) for part in parts]
        total = sum(jnp.sum(part, axis=1, keepdims=True) for part in parts)
        result = r_buf[:, :, at].reshape(2 * rows, HEAD_DIM).astype(F32)
        attended = None
        for dist in range(3):
            value = kv_buf[dist, h, 1].reshape(2 * rows, HEAD_DIM)
            term = jnp.dot((parts[dist] / total).astype(BF16), value, preferred_element_type=F32)
            attended = term if attended is None else attended + term
        stream = (result + attended).astype(BF16)
        line[h][z] = stream.reshape(2, rows, HEAD_DIM)
        pl.when(line_up)(lambda: line_copy(0, z, h).start())
        pl.when(line_dn)(lambda: line_copy(1, z, h).start())
        unsent.append((line_up, line_copy(0, z, h)))
        unsent.append((line_dn, line_copy(1, z, h)))

    def end_copy(h):
        return remote(end_out[h], end_in[h], end_s.at[h], end_r.at[h], dev_edge)

    def pick(flag, a, b):
        mask = jnp.full(a.shape, flag.astype(jnp.int32), jnp.int32) > 0
        return jnp.where(mask, a.astype(F32), b.astype(F32)).astype(BF16)

    def spread(h):
        for step in range(1, planes):
            below, above = z - step, z + step
            from_below = (below >= 0) & (z < planes - 1)
            from_above = (above < planes) & (z > 0)

            @pl.when(from_below)
            def _():
                line_copy(0, below, h).wait_recv()
                pl.when(line_up)(lambda: line_copy(0, below, h).start())

            @pl.when(from_above)
            def _():
                line_copy(1, above, h).wait_recv()
                pl.when(line_dn)(lambda: line_copy(1, above, h).start())

            unsent.append((from_below & line_up, line_copy(0, below, h)))
            unsent.append((from_above & line_dn, line_copy(1, above, h)))

        @pl.when(by_edge)
        def _():
            for r in range(most):
                end_out[h][r] = line[h][chosen_edge[r] // 2, chosen_edge[r] % 2]
            end_copy(h).start()

        unsent.append((by_edge, end_copy(h)))

        @pl.when(at_edge)
        def _():
            end_copy(h).wait_recv()
            for r in range(most):
                x_buf[y, t, h, pl.ds(r * rows, rows)] = pick(
                    chosen[r] // 2 == z, line[h][z, chosen[r] % 2], end_in[h][r]
                )

        @pl.when(jnp.logical_not(at_edge))
        def _():
            for r in range(most):
                x_buf[y, t, h, pl.ds(r * rows, rows)] = line[h][chosen[r] // 2, chosen[r] % 2]

    def gatherer(buf, sends, recvs, h):
        middle = buf.shape[3] // 2
        low, high, whole = pl.ds(0, middle), pl.ds(middle, middle), pl.ds(0, 2 * middle)

        def piece(i, at, device):
            ref = buf.at[at[0], at[1], h, at[2]]
            return remote(ref, ref, sends.at[i, h], recvs.at[i, h], device)

        def send(i, at, device):
            piece(i, at, device).start()
            unsent.append((None, piece(i, at, device)))

        def take(i, at):
            piece(i, at, dev_c).wait_recv()

        def first():
            send(0, (y, t, low), dev_x)
            send(1, (y, t, high), dev_y)
            send(2, (y, t, high), dev_x)
            send(3, (y, t, low), dev_y)
            send(4, (y, t, whole), dev_c)

        def second():
            take(0, (y, tx, low))
            send(5, (y, tx, low), dev_y)
            send(7, (y, tx, low), dev_c)
            take(1, (yo, t, high))
            send(6, (yo, t, high), dev_x)
            send(8, (yo, t, high), dev_c)
            take(2, (y, tx, high))
            send(9, (y, tx, high), dev_c)
            take(3, (yo, t, low))
            send(10, (yo, t, low), dev_c)

        def third():
            take(5, (yo, tx, low))
            send(11, (yo, tx, low), dev_c)
            take(6, (yo, tx, high))
            send(12, (yo, tx, high), dev_c)

        def near():
            take(4, (y, tc, whole))
            take(7, (y, txc, low))
            take(9, (y, txc, high))
            take(8, (yo, tc, high))
            take(10, (yo, tc, low))

        def far():
            take(11, (yo, txc, low))
            take(12, (yo, txc, high))

        return first, second, third, near, far

    def expert_parts(parts, pair):
        left, right = [], []
        square = square_buf[...]
        for py, pt in parts:
            for h in (2 * pair, 2 * pair + 1):
                start = pl.multiple_of((2 * pt + py) * half + h * HEAD_DIM, HEAD_DIM)
                x = x_buf[py, pt, h].astype(F32)
                square = square + jnp.sum(x * x, axis=1, keepdims=True)
                left.append((x * gain_ref[:, pl.ds(start, HEAD_DIM)]).astype(BF16))
                right.append(w_buf[pl.ds(start, HEAD_DIM), :])
        square_buf[...] = square
        acc_buf[...] += jnp.dot(
            jnp.concatenate(left, axis=1),
            jnp.concatenate(right, axis=0),
            preferred_element_type=F32,
        )

    stages = [gatherer(x_buf, feat_s, feat_r, h) for h in range(heads)]
    most_parts = [(y, t), (y, tc), (y, tx), (yo, t), (y, txc), (yo, tc)]
    rest_parts = [(yo, tx), (yo, txc)]
    for h in range(heads):
        kv_own(h)
    kv_relay(0)
    for i in (2 * heads, 2 * heads + 1):
        stay[i].wait()
        landed[i].wait_recv()
    for turn in range(heads + 3):
        if turn + 1 < heads:
            kv_relay(turn + 1)
        if turn < heads:
            attend(turn)
        if turn == heads:
            acc_buf[...] = jnp.zeros_like(acc_buf)
            square_buf[...] = jnp.zeros_like(square_buf)
            for copy in stay[2 * heads + 2 :]:
                copy.wait()
        if 0 <= turn - 1 < heads:
            spread(turn - 1)
            stages[turn - 1][0]()
        if 0 <= turn - 2 < heads:
            stages[turn - 2][1]()
        if 0 <= turn - 3 < heads:
            h = turn - 3
            if h == heads - 1:
                stages[h][3]()
                expert_parts(most_parts, h // 2)
            stages[h][2]()
            if h < heads - 1:
                stages[h][3]()
            stages[h][4]()
            if h == heads - 1:
                expert_parts(rest_parts, h // 2)
            elif h % 2 == 1:
                expert_parts(most_parts + rest_parts, h // 2)
    units = gate_ref.shape[2]
    features = gain_ref.shape[1]
    scale = lax.rsqrt(square_buf[...] * (1.0 / features) + epsilon)
    gate_val = acc_buf[:, pl.ds(0, units)] * scale
    up_val = acc_buf[:, pl.ds(units, units)] * scale
    hid_buf[y, t, 0] = (gate_val / (1.0 + jnp.exp(-gate_val)) * up_val).astype(BF16)
    for stage in gatherer(hid_buf, hid_s, hid_r, 0):
        stage()

    chunks = len(mix)
    span = half // chunks
    per = span // HEAD_DIM

    def edge_copy(way, c):
        dst = end_up[c] if way == 0 else end_dn[c]
        return remote(
            mix[c], dst, edge_s.at[way, c], edge_r.at[way, c], dev_up if way == 0 else dev_dn
        )

    def ret_copy(way, d, c):
        out, arrived = (up_out, up_in) if way == 0 else (dn_out, dn_in)
        return remote(
            out.at[c, d],
            arrived.at[c, d],
            ret_s.at[way, d, c],
            ret_r.at[way, d, c],
            dev_up if way == 0 else dev_dn,
        )

    landed[2 * heads + 2].wait_recv()
    hidden = [
        jnp.concatenate([hid_buf[h, i, 0] for i in range(hid_buf.shape[1])], axis=1)
        for h in range(2)
    ]
    for c in range(chunks):
        total = jnp.concatenate(
            [x_buf[y, t, c * per + i] for i in range(per)], axis=1
        ).astype(F32)
        for h in range(2):
            weight = down_buf[h + 2 * ((y + h) % 2), :, pl.ds(c * span, span)]
            branch = jnp.dot(hidden[h], weight, preferred_element_type=F32).astype(BF16)
            total = total + branch.astype(F32)
        mix[c][...] = total.astype(BF16).reshape(most, rows, span)
        pl.when(z == 0)(lambda: edge_copy(0, c).start())
        pl.when(z == planes - 1)(lambda: edge_copy(1, c).start())
        unsent.append((z == 0, edge_copy(0, c)))
        unsent.append((z == planes - 1, edge_copy(1, c)))

    for c in range(chunks):
        pl.when(z == 1)(lambda: edge_copy(0, c).wait_recv())
        pl.when(z == planes - 2)(lambda: edge_copy(1, c).wait_recv())
        for step in range(planes - 1):
            for way, d in ((0, planes - 1 - step), (1, step)):
                passes = (z < d) & (z > 0) if way == 0 else (z > d) & (z < planes - 1)
                near = z == 1 if way == 0 else z == planes - 2
                end = end_up[c] if way == 0 else end_dn[c]
                out, arrived = (up_out, up_in) if way == 0 else (dn_out, dn_in)

                @pl.when(passes & near)
                def _():
                    for n in range(2):
                        b = 2 * d + n
                        out[c, d, n] = pick(expert[b] == z, mix[c][slot[b]], end[slot[b]])

                @pl.when(passes & jnp.logical_not(near))
                def _():
                    ret_copy(way, d, c).wait_recv()
                    for n in range(2):
                        b = 2 * d + n
                        out[c, d, n] = pick(expert[b] == z, mix[c][slot[b]], arrived[c, d, n])

                pl.when(passes)(lambda: ret_copy(way, d, c).start())
                unsent.append((passes, ret_copy(way, d, c)))

    def finish(which, c):
        return pl.ds(pl.multiple_of(which * half + c * span, span), span)

    def last_copy(c):
        return remote(
            fin_buf.at[c, yo], out_ref.at[:, finish(y, c)], last_s.at[c], last_r.at[c], dev_y
        )

    for c in range(chunks):
        for d in range(planes):

            @pl.when(z == d)
            def _():
                if d > 1:
                    ret_copy(0, d, c).wait_recv()
                if d < planes - 2:
                    ret_copy(1, d, c).wait_recv()
                for n in range(2):
                    b = 2 * d + n
                    value = mix[c][slot[b]]
                    if d > 0:
                        value = pick(
                            expert[b] < z, up_in[c, d, n] if d > 1 else end_up[c][slot[b]], value
                        )
                    if d < planes - 1:
                        value = pick(
                            expert[b] > z,
                            dn_in[c, d, n] if d < planes - 2 else end_dn[c][slot[b]],
                            value,
                        )
                    fin_buf[c, n] = value

        last_copy(c).start()
        unsent.append((None, last_copy(c)))
        out_ref[:, finish(y, c)] = fin_buf[c, y]
    for c in range(chunks):
        mine = out_ref.at[:, finish(yo, c)]
        remote(mine, mine, last_s.at[c], last_r.at[c], dev_y).wait_recv()
    for flag, copy in unsent:
        if flag is None:
            copy.wait_send()
        else:
            pl.when(flag)(lambda: copy.wait_send())


def local(
    queries, keys, values, residual_in, norm_gain, routing, gate_weight, up_weight, down_weight
):
    seq_count = lax.axis_size("seq")
    tp_count = lax.axis_size("tp")
    rows, width = queries.shape
    units = gate_weight.shape[2]
    planes = seq_count // 2
    fits = (
        tp_count == 4
        and seq_count % 2 == 0
        and 4 <= planes <= 8
        and rows == BLOCK
        and WINDOW == 4 * rows
        and units == 128
        and width % (8 * HEAD_DIM) == 0
    )
    if not fits:
        return local_general(
            queries,
            keys,
            values,
            residual_in,
            norm_gain,
            routing,
            gate_weight,
            up_weight,
            down_weight,
        )
    half = width // 2
    heads = half // HEAD_DIM
    most = min(2 * seq_count // planes, seq_count - planes + 1)
    chunks = 2
    span = half // chunks
    vmem = pl.BlockSpec(memory_space=pltpu.VMEM)
    anywhere = pl.BlockSpec(memory_space=pl.ANY)
    dma = pltpu.SemaphoreType.DMA

    def room(*shape, kind=BF16):
        return pltpu.VMEM(shape, kind)

    scratch = (
        room(2, rows, half),
        room(2, rows, half),
        room(3, heads, 2, 2, rows, HEAD_DIM),
        [room(planes, 2, rows, HEAD_DIM) for _ in range(heads)],
        [room(most, rows, HEAD_DIM) for _ in range(heads)],
        [room(most, rows, HEAD_DIM) for _ in range(heads)],
        room(2, tp_count, heads, most * rows, HEAD_DIM),
        room(norm_gain.shape[0], 2 * units),
        room(most * rows, 2 * units, kind=F32),
        room(most * rows, 1, kind=F32),
        room(2, tp_count, 1, most * rows, units),
        room(4, down_weight.shape[1], half),
        [room(most, rows, span) for _ in range(chunks)],
        [room(most, rows, span) for _ in range(chunks)],
        [room(most, rows, span) for _ in range(chunks)],
        room(chunks, planes, 2, rows, span),
        room(chunks, planes, 2, rows, span),
        room(chunks, planes, 2, rows, span),
        room(chunks, planes, 2, rows, span),
        room(chunks, 2, rows, span),
        dma((2 * heads + 3,)),
        dma((2 * heads + 3,)),
        dma((2 * heads + 5,)),
        dma((2, heads)),
        dma((2, heads)),
        dma((2, planes, heads)),
        dma((2, planes, heads)),
        dma((heads,)),
        dma((heads,)),
        dma((13, heads)),
        dma((13, heads)),
        dma((13, 1)),
        dma((13, 1)),
        dma((2, planes, chunks)),
        dma((2, planes, chunks)),
        dma((2, chunks)),
        dma((2, chunks)),
        dma((chunks,)),
        dma((chunks,)),
    )
    flat, tree = jax.tree.flatten(scratch, is_leaf=lambda leaf: not isinstance(leaf, (list, tuple)))

    def kernel(*refs):
        layer_kernel(planes, most, refs[:9], refs[9], jax.tree.unflatten(tree, refs[10:]))

    return pl.pallas_call(
        kernel,
        name="layer",
        out_shape=jax.ShapeDtypeStruct((rows, width), BF16),
        in_specs=[pl.BlockSpec(memory_space=pltpu.SMEM)]
        + [anywhere] * 4
        + [vmem]
        + [anywhere] * 3,
        out_specs=vmem,
        scratch_shapes=flat,
        compiler_params=pltpu.CompilerParams(
            collective_id=0, has_side_effects=True, vmem_limit_bytes=48 * 1024 * 1024
        ),
    )(
        routing,
        queries,
        keys,
        values,
        residual_in,
        norm_gain.reshape(1, -1),
        gate_weight,
        up_weight,
        down_weight,
    )


def solution(mesh):
    in_specs = (
        P("seq", "tp"),
        P("seq", "tp"),
        P("seq", "tp"),
        P("seq", "tp"),
        P(),
        P(),
        P("seq", None, "tp"),
        P("seq", None, "tp"),
        P("seq", None, "tp"),
    )
    out_specs = P("seq", "tp")
    return jax.shard_map(local, mesh=mesh, in_specs=in_specs, out_specs=out_specs, check_vma=False)
```

```python
import math

import jax
import jax.numpy as jnp
from jax import lax
from jax.experimental import pallas as pl
from jax.experimental.pallas import tpu as pltpu
from jax.sharding import PartitionSpec as P

HEAD_DIM = 128
BLOCK = 128
WINDOW = 512


epsilon = 1e-05
masked_score = -1e30


def shifted(block, axis, distance):
    devices = range(lax.axis_size(axis))
    route = [(i - distance, i) for i in devices if i - distance in devices]
    return lax.ppermute(block, axis, route)


def local_general(
    queries, keys, values, residual_in, norm_gain, routing, gate_weight, up_weight, down_weight
):
    seq_count = lax.axis_size("seq")
    seq_place = lax.axis_index("seq")
    tok_rows = queries.shape[0]
    feat_width = queries.shape[1]
    head_count = feat_width // HEAD_DIM
    prior_count = (WINDOW - 1) // tok_rows + 1
    earlier_keys = []
    earlier_values = []
    for distance in range(1, prior_count + 1):
        moved_keys, moved_values = shifted((keys, values), "seq", distance)
        earlier_keys.insert(0, moved_keys)
        earlier_values.insert(0, moved_values)
    key_all = jnp.concatenate(earlier_keys + [keys], axis=0).reshape(-1, head_count, HEAD_DIM)
    value_all = jnp.concatenate(earlier_values + [values], axis=0).reshape(-1, head_count, HEAD_DIM)
    query_heads = queries.reshape(tok_rows, head_count, HEAD_DIM)
    query_pos = seq_place * tok_rows + jnp.arange(tok_rows, dtype=jnp.int32)
    key_pos = (
        seq_place * tok_rows
        - prior_count * tok_rows
        + jnp.arange((prior_count + 1) * tok_rows, dtype=jnp.int32)
    )
    visible = (
        (key_pos[None, :] >= 0)
        & (key_pos[None, :] <= query_pos[:, None])
        & (key_pos[None, :] > query_pos[:, None] - WINDOW)
    )
    scores = jnp.einsum(
        "qhd,khd->hqk", query_heads, key_all, preferred_element_type=jnp.float32
    ) * (1.0 / math.sqrt(HEAD_DIM))
    scores = jnp.where(visible[None], scores, masked_score)
    top_score = jnp.max(scores, axis=2, keepdims=True)
    expo = jnp.exp(scores - top_score)
    weights_soft = (expo / jnp.sum(expo, axis=2, keepdims=True)).astype(jnp.bfloat16)
    attended = jnp.einsum(
        "hqk,khd->qhd", weights_soft, value_all, preferred_element_type=jnp.float32
    ).reshape(tok_rows, feat_width)
    stream = (residual_in.astype(jnp.float32) + attended).astype(jnp.bfloat16)
    send_width = stream.shape[1]
    blocks_dev = tok_rows // BLOCK
    piece_rows = BLOCK // seq_count
    spread_in = stream.reshape(blocks_dev, seq_count, piece_rows, send_width)
    spread_out = lax.all_to_all(spread_in, "seq", split_axis=1, concat_axis=0, tiled=True)
    block_count = blocks_dev * seq_count
    spread_rows = spread_out.reshape(block_count, piece_rows, send_width)
    expert_ids = routing[:, 0]
    expert_count = seq_count // 2
    most_blocks = min(2 * block_count // expert_count, block_count - expert_count + 1)
    order_index = jnp.arange(block_count, dtype=jnp.int32)
    same_expert = expert_ids[None, :] == expert_ids[:, None]
    rank_of = jnp.sum(same_expert & (order_index[None, :] < order_index[:, None]), axis=1)
    expert_range = jnp.arange(expert_count, dtype=jnp.int32)
    slot_range = jnp.arange(most_blocks, dtype=jnp.int32)
    selector = (
        (expert_ids[None, None, :] == expert_range[:, None, None])
        & (rank_of[None, None, :] == slot_range[None, :, None])
    ).astype(jnp.bfloat16)
    picked = jnp.einsum(
        "erb,bqf->erqf", selector, spread_rows, preferred_element_type=jnp.float32
    ).astype(jnp.bfloat16)
    outgoing = jnp.broadcast_to(
        picked[:, None], (expert_count, 2, most_blocks, piece_rows, send_width)
    )
    outgoing = outgoing.reshape(seq_count, most_blocks, piece_rows, send_width)
    features_full = lax.all_gather(
        lax.all_to_all(outgoing, "seq", split_axis=0, concat_axis=0, tiled=True),
        "tp",
        axis=3,
        tiled=True,
    )
    source_count = features_full.shape[0]
    slot_count = features_full.shape[1]
    stream_f32 = features_full.astype(jnp.float32)
    mean_square = jnp.mean(stream_f32 * stream_f32, axis=3, keepdims=True)
    normed = (stream_f32 * lax.rsqrt(mean_square + epsilon) * norm_gain).astype(jnp.bfloat16)
    normed = normed.reshape(-1, normed.shape[3])
    gate_val = jnp.dot(normed, gate_weight[0], preferred_element_type=jnp.float32)
    up_val = jnp.dot(normed, up_weight[0], preferred_element_type=jnp.float32)
    hidden = (jax.nn.silu(gate_val) * up_val).astype(jnp.bfloat16)
    hidden_half = lax.all_gather(hidden, "tp", axis=1, tiled=True)
    partial_value = jnp.dot(hidden_half, down_weight[0], preferred_element_type=jnp.float32).astype(
        jnp.bfloat16
    )
    partial_value = partial_value.reshape(source_count, slot_count, piece_rows, feat_width)
    returned = lax.all_to_all(partial_value, "seq", split_axis=0, concat_axis=0, tiled=True)
    returned = returned.reshape(expert_count, 2, most_blocks, piece_rows * feat_width)
    combined = jnp.einsum("erb,epry->pby", selector, returned, preferred_element_type=jnp.float32)
    residual_rows = spread_rows
    residual_rows = residual_rows.reshape(block_count, piece_rows * feat_width).astype(jnp.float32)
    finished = (residual_rows + combined[0] + combined[1]).astype(jnp.bfloat16)
    finished = finished.reshape(seq_count, blocks_dev, piece_rows, feat_width)
    restored = lax.all_to_all(finished, "seq", split_axis=0, concat_axis=2, tiled=True)
    return restored.reshape(tok_rows, feat_width)


BF16 = jnp.bfloat16
F32 = jnp.float32


def remote(src, dst, send_sem, recv_sem, device):
    return pltpu.make_async_remote_copy(
        src_ref=src,
        dst_ref=dst,
        send_sem=send_sem,
        recv_sem=recv_sem,
        device_id=device,
        device_id_type=pl.DeviceIdType.MESH,
    )


def layer_kernel(planes, most, arguments, out_ref, scratch):
    (
        routing_ref, q_ref, k_ref, v_ref, r_ref, gain_ref, gate_ref, up_ref, down_ref
    ) = arguments
    (
        q_buf,
        r_buf,
        kv_buf,
        line,
        end_out,
        end_in,
        x_buf,
        w_buf,
        acc_buf,
        square_buf,
        hid_buf,
        down_buf,
        mix,
        end_up,
        end_dn,
        up_out,
        up_in,
        dn_out,
        dn_in,
        fin_buf,
        pair_s,
        pair_r,
        local_s,
        kvline_s,
        kvline_r,
        line_s,
        line_r,
        end_s,
        end_r,
        feat_s,
        feat_r,
        hid_s,
        hid_r,
        ret_s,
        ret_r,
        edge_s,
        edge_r,
        last_s,
        last_r,
    ) = scratch
    rows = q_ref.shape[0]
    half = q_ref.shape[1] // 2
    heads = half // HEAD_DIM
    blocks = 2 * planes
    me = lax.axis_index("seq")
    t = lax.axis_index("tp")
    z = me // 2
    y = me % 2
    yo = 1 - y
    mate = 2 * z + yo
    tc = t + 1 - 2 * (t % 2)
    tx = t + 2 - 4 * (t // 2)
    txc = tx + 1 - 2 * (tx % 2)
    dev_y, dev_c, dev_x = (mate, t), (me, tc), (me, tx)
    dev_up, dev_dn = (me + 2, t), (me - 2, t)
    has_up, has_dn = z < planes - 1, z > 0
    unsent = []

    barrier = pltpu.get_barrier_semaphore()

    def greet(device):
        pl.semaphore_signal(
            barrier, inc=1, device_id=device, device_id_type=pl.DeviceIdType.MESH
        )

    for device in (dev_y, dev_c, dev_x):
        greet(device)
    pl.when(has_up)(lambda: greet(dev_up))
    pl.when(has_dn)(lambda: greet(dev_dn))

    def cols(which, h):
        return pl.ds(pl.multiple_of(which * half + h * HEAD_DIM, HEAD_DIM), HEAD_DIM)

    def wide(which):
        return pl.ds(pl.multiple_of(which * half, half), half)

    stay = []
    for h in range(heads):
        stay.append((k_ref.at[:, cols(y, h)], kv_buf.at[0, h, 0, y]))
        stay.append((v_ref.at[:, cols(y, h)], kv_buf.at[0, h, 1, y]))
    stay.append((q_ref.at[:, wide(y)], q_buf.at[y]))
    stay.append((r_ref.at[:, wide(y)], r_buf.at[y]))
    stay.append((gate_ref.at[0], w_buf.at[:, pl.ds(0, gate_ref.shape[2])]))
    stay.append((up_ref.at[0], w_buf.at[:, pl.ds(gate_ref.shape[2], gate_ref.shape[2])]))
    stay.append((down_ref.at[0, :, wide(y)], down_buf.at[y]))
    stay = [pltpu.make_async_copy(a, b, local_s.at[i]) for i, (a, b) in enumerate(stay)]
    for copy in stay:
        copy.start()

    expert = [routing_ref[b, 0] for b in range(blocks)]
    slot = []
    for b in range(blocks):
        count = jnp.int32(0)
        for j in range(b):
            count = count + jnp.where(expert[j] == expert[b], 1, 0)
        slot.append(jnp.minimum(count, most - 1))

    def listing(which):
        found = []
        for r in range(most):
            index = jnp.int32(0)
            for b in range(blocks):
                index = jnp.where((expert[b] == which) & (slot[b] == r), b, index)
            found.append(index)
        return found

    chosen = listing(z)
    at_edge = (z == 0) | (z == planes - 1)
    by_edge = (z == 1) | (z == planes - 2)
    chosen_edge = listing(jnp.where(z == 1, 0, planes - 1))
    dev_edge = (jnp.where(z == 1, me - 2, me + 2), t)
    line_up, line_dn = z < planes - 2, z > 1

    for dist in (1, 2):

        @pl.when(z < dist)
        def _():
            kv_buf[dist] = jnp.zeros(kv_buf.shape[1:], kv_buf.dtype)

    pl.semaphore_wait(
        barrier, 3 + jnp.where(has_up, 1, 0) + jnp.where(has_dn, 1, 0)
    )

    def pair_copy(i, src, dst):
        return remote(src, dst, pair_s.at[i], pair_r.at[i], dev_y)

    swap, landed = [], []
    for h in range(heads):
        for n, ref in enumerate((k_ref, v_ref)):
            i = len(swap)
            swap.append(pair_copy(i, ref.at[:, cols(yo, h)], kv_buf.at[0, h, n, y]))
            landed.append(pair_copy(i, kv_buf.at[0, h, n, yo], kv_buf.at[0, h, n, yo]))
    for ref, buf in ((q_ref, q_buf), (r_ref, r_buf)):
        i = len(swap)
        swap.append(pair_copy(i, ref.at[:, wide(yo)], buf.at[y]))
        landed.append(pair_copy(i, buf.at[yo], buf.at[yo]))
    i = len(swap)
    swap.append(pair_copy(i, down_ref.at[0, :, wide(yo)], down_buf.at[y + 2]))
    landed.append(pair_copy(i, down_buf.at[yo + 2], down_buf.at[yo + 2]))
    for copy in swap:
        copy.start()
        unsent.append((None, copy))

    def kv_copy(dist, h):
        return remote(
            kv_buf.at[dist, h],
            kv_buf.at[dist + 1, h],
            kvline_s.at[dist, h],
            kvline_r.at[dist, h],
            dev_up,
        )

    def kv_own(h):
        for i in (2 * h, 2 * h + 1):
            stay[i].wait()
            landed[i].wait_recv()
        pl.when(has_up)(lambda: kv_copy(0, h).start())
        unsent.append((has_up, kv_copy(0, h)))

    def kv_relay(h):
        pl.when(has_dn)(lambda: kv_copy(0, h).wait_recv())
        pl.when(has_dn & has_up)(lambda: kv_copy(1, h).start())
        unsent.append((has_dn & has_up, kv_copy(1, h)))

    def line_copy(way, plane, h):
        return remote(
            line[h].at[plane],
            line[h].at[plane],
            line_s.at[way, plane, h],
            line_r.at[way, plane, h],
            dev_up if way == 0 else dev_dn,
        )

    row_at = lax.broadcasted_iota(jnp.int32, (rows, rows), 0)
    col_at = lax.broadcasted_iota(jnp.int32, (rows, rows), 1)
    behind = [jnp.where(z >= dist, 0.0, masked_score).astype(F32) for dist in range(3)]

    def attend(h):
        pl.when(z > 1)(lambda: kv_copy(1, h).wait_recv())
        at = pl.ds(h * HEAD_DIM, HEAD_DIM)
        count = WINDOW // rows
        for n in range(2):
            query = q_buf[n, :, at]
            places = []
            for back in range(count + 1):
                dist = (back - n + 1) // 2
                places.append((dist, (n - back) % 2))
            parts = []
            for back, (dist, block) in enumerate(places):
                part = lax.dot_general(
                    query,
                    kv_buf[dist, h, 0, block],
                    (((1,), (1,)), ((), ())),
                    preferred_element_type=F32,
                )
                if back == 0:
                    part = jnp.where(col_at <= row_at, part, masked_score)
                if back == count:
                    part = jnp.where(col_at > row_at, part, masked_score)
                if dist > 0:
                    part = part + behind[dist]
                parts.append(part)
            top = parts[0]
            for part in parts[1:]:
                top = jnp.maximum(top, part)
            top = jnp.max(top, axis=1, keepdims=True)
            parts = [jnp.exp((part - top) * (1.0 / math.sqrt(HEAD_DIM))) for part in parts]
            total = parts[0]
            for part in parts[1:]:
                total = total + part
            share = 1.0 / jnp.sum(total, axis=1, keepdims=True)
            attended = jnp.dot(
                jnp.concatenate([(part * share).astype(BF16) for part in parts], axis=1),
                jnp.concatenate([kv_buf[dist, h, 1, block] for dist, block in places], axis=0),
                preferred_element_type=F32,
            )
            line[h][z, n] = (r_buf[n, :, at].astype(F32) + attended).astype(BF16)
        pl.when(line_up)(lambda: line_copy(0, z, h).start())
        pl.when(line_dn)(lambda: line_copy(1, z, h).start())
        unsent.append((line_up, line_copy(0, z, h)))
        unsent.append((line_dn, line_copy(1, z, h)))

    def end_copy(h):
        return remote(end_out[h], end_in[h], end_s.at[h], end_r.at[h], dev_edge)

    def pick(flag, a, b):
        mask = jnp.full(a.shape, flag.astype(jnp.int32), jnp.int32) > 0
        return jnp.where(mask, a.astype(F32), b.astype(F32)).astype(BF16)

    def spread(h):
        for step in range(1, planes):
            below, above = z - step, z + step
            from_below = (below >= 0) & (z < planes - 1)
            from_above = (above < planes) & (z > 0)

            @pl.when(from_below)
            def _():
                line_copy(0, below, h).wait_recv()
                pl.when(line_up)(lambda: line_copy(0, below, h).start())

            @pl.when(from_above)
            def _():
                line_copy(1, above, h).wait_recv()
                pl.when(line_dn)(lambda: line_copy(1, above, h).start())

            unsent.append((from_below & line_up, line_copy(0, below, h)))
            unsent.append((from_above & line_dn, line_copy(1, above, h)))

        @pl.when(by_edge)
        def _():
            for r in range(most):
                end_out[h][r] = line[h][chosen_edge[r] // 2, chosen_edge[r] % 2]
            end_copy(h).start()

        unsent.append((by_edge, end_copy(h)))

        @pl.when(at_edge)
        def _():
            end_copy(h).wait_recv()
            for r in range(most):
                x_buf[y, t, h, pl.ds(r * rows, rows)] = pick(
                    chosen[r] // 2 == z, line[h][z, chosen[r] % 2], end_in[h][r]
                )

        @pl.when(jnp.logical_not(at_edge))
        def _():
            for r in range(most):
                x_buf[y, t, h, pl.ds(r * rows, rows)] = line[h][chosen[r] // 2, chosen[r] % 2]

    def gatherer(buf, sends, recvs, h):
        middle = buf.shape[3] // 2
        low, high, whole = pl.ds(0, middle), pl.ds(middle, middle), pl.ds(0, 2 * middle)

        def piece(i, at, device):
            ref = buf.at[at[0], at[1], h, at[2]]
            return remote(ref, ref, sends.at[i, h], recvs.at[i, h], device)

        def send(i, at, device):
            piece(i, at, device).start()
            unsent.append((None, piece(i, at, device)))

        def take(i, at):
            piece(i, at, dev_c).wait_recv()

        def first():
            send(0, (y, t, low), dev_x)
            send(1, (y, t, high), dev_y)
            send(2, (y, t, high), dev_x)
            send(3, (y, t, low), dev_y)
            send(4, (y, t, whole), dev_c)

        def second():
            take(0, (y, tx, low))
            send(5, (y, tx, low), dev_y)
            send(7, (y, tx, low), dev_c)
            take(1, (yo, t, high))
            send(6, (yo, t, high), dev_x)
            send(8, (yo, t, high), dev_c)
            take(2, (y, tx, high))
            send(9, (y, tx, high), dev_c)
            take(3, (yo, t, low))
            send(10, (yo, t, low), dev_c)

        def third():
            take(5, (yo, tx, low))
            send(11, (yo, tx, low), dev_c)
            take(6, (yo, tx, high))
            send(12, (yo, tx, high), dev_c)

        def near():
            take(4, (y, tc, whole))
            take(7, (y, txc, low))
            take(9, (y, txc, high))
            take(8, (yo, tc, high))
            take(10, (yo, tc, low))

        def far():
            take(11, (yo, txc, low))
            take(12, (yo, txc, high))

        return first, second, third, near, far

    def expert_parts(parts, pair):
        left, right = [], []
        square = square_buf[...]
        for py, pt in parts:
            for h in (2 * pair, 2 * pair + 1):
                start = pl.multiple_of((2 * pt + py) * half + h * HEAD_DIM, HEAD_DIM)
                x = x_buf[py, pt, h].astype(F32)
                square = square + jnp.sum(x * x, axis=1, keepdims=True)
                left.append((x * gain_ref[:, pl.ds(start, HEAD_DIM)]).astype(BF16))
                right.append(w_buf[pl.ds(start, HEAD_DIM), :])
        square_buf[...] = square
        acc_buf[...] += jnp.dot(
            jnp.concatenate(left, axis=1),
            jnp.concatenate(right, axis=0),
            preferred_element_type=F32,
        )

    stages = [gatherer(x_buf, feat_s, feat_r, h) for h in range(heads)]
    most_parts = [(y, t), (y, tc), (y, tx), (yo, t), (y, txc), (yo, tc)]
    rest_parts = [(yo, tx), (yo, txc)]
    for h in range(heads):
        kv_own(h)
    kv_relay(0)
    for i in (2 * heads, 2 * heads + 1):
        stay[i].wait()
        landed[i].wait_recv()
    for turn in range(heads + 3):
        if turn + 1 < heads:
            kv_relay(turn + 1)
        if turn < heads:
            attend(turn)
        if turn == heads:
            acc_buf[...] = jnp.zeros_like(acc_buf)
            square_buf[...] = jnp.zeros_like(square_buf)
            for copy in stay[2 * heads + 2 :]:
                copy.wait()
        if 0 <= turn - 1 < heads:
            spread(turn - 1)
            stages[turn - 1][0]()
        if 0 <= turn - 2 < heads:
            stages[turn - 2][1]()
        if 0 <= turn - 3 < heads:
            h = turn - 3
            if h == heads - 1:
                stages[h][3]()
                expert_parts(most_parts, h // 2)
            stages[h][2]()
            if h < heads - 1:
                stages[h][3]()
            stages[h][4]()
            if h == heads - 1:
                expert_parts(rest_parts, h // 2)
            elif h % 2 == 1:
                expert_parts(most_parts + rest_parts, h // 2)
    units = gate_ref.shape[2]
    features = gain_ref.shape[1]
    scale = lax.rsqrt(square_buf[...] * (1.0 / features) + epsilon)
    gate_val = acc_buf[:, pl.ds(0, units)] * scale
    up_val = acc_buf[:, pl.ds(units, units)] * scale
    hid_buf[y, t, 0] = (gate_val / (1.0 + jnp.exp(-gate_val)) * up_val).astype(BF16)
    for stage in gatherer(hid_buf, hid_s, hid_r, 0):
        stage()

    chunks = len(mix)
    span = half // chunks
    per = span // HEAD_DIM

    def edge_copy(way, c):
        dst = end_up[c] if way == 0 else end_dn[c]
        return remote(
            mix[c], dst, edge_s.at[way, c], edge_r.at[way, c], dev_up if way == 0 else dev_dn
        )

    def ret_copy(way, d, c):
        out, arrived = (up_out, up_in) if way == 0 else (dn_out, dn_in)
        return remote(
            out.at[c, d],
            arrived.at[c, d],
            ret_s.at[way, d, c],
            ret_r.at[way, d, c],
            dev_up if way == 0 else dev_dn,
        )

    landed[2 * heads + 2].wait_recv()
    hidden = [
        jnp.concatenate([hid_buf[h, i, 0] for i in range(hid_buf.shape[1])], axis=1)
        for h in range(2)
    ]
    for c in range(chunks):
        total = jnp.concatenate(
            [x_buf[y, t, c * per + i] for i in range(per)], axis=1
        ).astype(F32)
        for h in range(2):
            weight = down_buf[h + 2 * ((y + h) % 2), :, pl.ds(c * span, span)]
            branch = jnp.dot(hidden[h], weight, preferred_element_type=F32).astype(BF16)
            total = total + branch.astype(F32)
        mix[c][...] = total.astype(BF16).reshape(most, rows, span)
        pl.when(z == 0)(lambda: edge_copy(0, c).start())
        pl.when(z == planes - 1)(lambda: edge_copy(1, c).start())
        unsent.append((z == 0, edge_copy(0, c)))
        unsent.append((z == planes - 1, edge_copy(1, c)))

    def relay(c, close):
        if close:
            pl.when(z == 1)(lambda: edge_copy(0, c).wait_recv())
            pl.when(z == planes - 2)(lambda: edge_copy(1, c).wait_recv())
        for step in range(planes - 1):
            for way, d in ((0, planes - 1 - step), (1, step)):
                passes = (z < d) & (z > 0) if way == 0 else (z > d) & (z < planes - 1)
                near = z == 1 if way == 0 else z == planes - 2
                end = end_up[c] if way == 0 else end_dn[c]
                out, arrived = (up_out, up_in) if way == 0 else (dn_out, dn_in)
                here = passes & near if close else passes & jnp.logical_not(near)

                @pl.when(here)
                def _():
                    if not close:
                        ret_copy(way, d, c).wait_recv()
                    for n in range(2):
                        b = 2 * d + n
                        other = end[slot[b]] if close else arrived[c, d, n]
                        out[c, d, n] = pick(expert[b] == z, mix[c][slot[b]], other)
                    ret_copy(way, d, c).start()

                unsent.append((here, ret_copy(way, d, c)))

    def finish(which, c):
        return pl.ds(pl.multiple_of(which * half + c * span, span), span)

    def last_copy(c):
        return remote(
            fin_buf.at[c, yo], out_ref.at[:, finish(y, c)], last_s.at[c], last_r.at[c], dev_y
        )

    def arrive(c):
        for d in range(planes):

            @pl.when(z == d)
            def _():
                if d > 1:
                    ret_copy(0, d, c).wait_recv()
                if d < planes - 2:
                    ret_copy(1, d, c).wait_recv()
                for n in range(2):
                    b = 2 * d + n
                    value = mix[c][slot[b]]
                    if d > 0:
                        value = pick(
                            expert[b] < z, up_in[c, d, n] if d > 1 else end_up[c][slot[b]], value
                        )
                    if d < planes - 1:
                        value = pick(
                            expert[b] > z,
                            dn_in[c, d, n] if d < planes - 2 else end_dn[c][slot[b]],
                            value,
                        )
                    fin_buf[c, n] = value

        last_copy(c).start()
        unsent.append((None, last_copy(c)))
        out_ref[:, finish(y, c)] = fin_buf[c, y]
    relay(0, True)
    for c in range(chunks):
        if c + 1 < chunks:
            relay(c + 1, True)
        relay(c, False)
        if c > 0:
            arrive(c - 1)
    arrive(chunks - 1)
    for c in range(chunks):
        mine = out_ref.at[:, finish(yo, c)]
        remote(mine, mine, last_s.at[c], last_r.at[c], dev_y).wait_recv()
    for flag, copy in unsent:
        if flag is None:
            copy.wait_send()
        else:
            pl.when(flag)(lambda: copy.wait_send())


def local(
    queries, keys, values, residual_in, norm_gain, routing, gate_weight, up_weight, down_weight
):
    seq_count = lax.axis_size("seq")
    tp_count = lax.axis_size("tp")
    rows, width = queries.shape
    units = gate_weight.shape[2]
    planes = seq_count // 2
    fits = (
        tp_count == 4
        and seq_count % 2 == 0
        and 4 <= planes <= 8
        and rows == BLOCK
        and WINDOW == 4 * rows
        and units == 128
        and width % (8 * HEAD_DIM) == 0
    )
    if not fits:
        return local_general(
            queries,
            keys,
            values,
            residual_in,
            norm_gain,
            routing,
            gate_weight,
            up_weight,
            down_weight,
        )
    half = width // 2
    heads = half // HEAD_DIM
    most = min(2 * seq_count // planes, seq_count - planes + 1)
    chunks = 4
    span = half // chunks
    vmem = pl.BlockSpec(memory_space=pltpu.VMEM)
    anywhere = pl.BlockSpec(memory_space=pltpu.MemorySpace.HBM)
    dma = pltpu.SemaphoreType.DMA

    def room(*shape, kind=BF16):
        return pltpu.VMEM(shape, kind)

    scratch = (
        room(2, rows, half),
        room(2, rows, half),
        room(3, heads, 2, 2, rows, HEAD_DIM),
        [room(planes, 2, rows, HEAD_DIM) for _ in range(heads)],
        [room(most, rows, HEAD_DIM) for _ in range(heads)],
        [room(most, rows, HEAD_DIM) for _ in range(heads)],
        room(2, tp_count, heads, most * rows, HEAD_DIM),
        room(norm_gain.shape[0], 2 * units),
        room(most * rows, 2 * units, kind=F32),
        room(most * rows, 1, kind=F32),
        room(2, tp_count, 1, most * rows, units),
        room(4, down_weight.shape[1], half),
        [room(most, rows, span) for _ in range(chunks)],
        [room(most, rows, span) for _ in range(chunks)],
        [room(most, rows, span) for _ in range(chunks)],
        room(chunks, planes, 2, rows, span),
        room(chunks, planes, 2, rows, span),
        room(chunks, planes, 2, rows, span),
        room(chunks, planes, 2, rows, span),
        room(chunks, 2, rows, span),
        dma((2 * heads + 3,)),
        dma((2 * heads + 3,)),
        dma((2 * heads + 5,)),
        dma((2, heads)),
        dma((2, heads)),
        dma((2, planes, heads)),
        dma((2, planes, heads)),
        dma((heads,)),
        dma((heads,)),
        dma((13, heads)),
        dma((13, heads)),
        dma((13, 1)),
        dma((13, 1)),
        dma((2, planes, chunks)),
        dma((2, planes, chunks)),
        dma((2, chunks)),
        dma((2, chunks)),
        dma((chunks,)),
        dma((chunks,)),
    )
    flat, tree = jax.tree.flatten(scratch, is_leaf=lambda leaf: not isinstance(leaf, (list, tuple)))

    def kernel(*refs):
        layer_kernel(planes, most, refs[:9], refs[9], jax.tree.unflatten(tree, refs[10:]))

    return pl.pallas_call(
        kernel,
        name="layer",
        out_shape=jax.ShapeDtypeStruct((rows, width), BF16),
        in_specs=[pl.BlockSpec(memory_space=pltpu.SMEM)]
        + [anywhere] * 4
        + [vmem]
        + [anywhere] * 3,
        out_specs=vmem,
        scratch_shapes=flat,
        compiler_params=pltpu.CompilerParams(
            collective_id=0, has_side_effects=True, vmem_limit_bytes=48 * 1024 * 1024
        ),
    )(
        routing,
        queries,
        keys,
        values,
        residual_in,
        norm_gain.reshape(1, -1),
        gate_weight,
        up_weight,
        down_weight,
    )


def solution(mesh):
    in_specs = (
        P("seq", "tp"),
        P("seq", "tp"),
        P("seq", "tp"),
        P("seq", "tp"),
        P(),
        P(),
        P("seq", None, "tp"),
        P("seq", None, "tp"),
        P("seq", None, "tp"),
    )
    out_specs = P("seq", "tp")
    return jax.shard_map(local, mesh=mesh, in_specs=in_specs, out_specs=out_specs, check_vma=False)
```

```python
import math

import jax
import jax.numpy as jnp
from jax import lax
from jax.experimental import pallas as pl
from jax.experimental.pallas import tpu as pltpu
from jax.sharding import PartitionSpec as P

HEAD_DIM = 128
BLOCK = 128
WINDOW = 512


epsilon = 1e-05
masked_score = -1e30


def shifted(block, axis, distance):
    devices = range(lax.axis_size(axis))
    route = [(i - distance, i) for i in devices if i - distance in devices]
    return lax.ppermute(block, axis, route)


def local_general(
    queries, keys, values, residual_in, norm_gain, routing, gate_weight, up_weight, down_weight
):
    seq_count = lax.axis_size("seq")
    seq_place = lax.axis_index("seq")
    tok_rows = queries.shape[0]
    feat_width = queries.shape[1]
    head_count = feat_width // HEAD_DIM
    prior_count = (WINDOW - 1) // tok_rows + 1
    earlier_keys = []
    earlier_values = []
    for distance in range(1, prior_count + 1):
        moved_keys, moved_values = shifted((keys, values), "seq", distance)
        earlier_keys.insert(0, moved_keys)
        earlier_values.insert(0, moved_values)
    key_all = jnp.concatenate(earlier_keys + [keys], axis=0).reshape(-1, head_count, HEAD_DIM)
    value_all = jnp.concatenate(earlier_values + [values], axis=0).reshape(-1, head_count, HEAD_DIM)
    query_heads = queries.reshape(tok_rows, head_count, HEAD_DIM)
    query_pos = seq_place * tok_rows + jnp.arange(tok_rows, dtype=jnp.int32)
    key_pos = (
        seq_place * tok_rows
        - prior_count * tok_rows
        + jnp.arange((prior_count + 1) * tok_rows, dtype=jnp.int32)
    )
    visible = (
        (key_pos[None, :] >= 0)
        & (key_pos[None, :] <= query_pos[:, None])
        & (key_pos[None, :] > query_pos[:, None] - WINDOW)
    )
    scores = jnp.einsum(
        "qhd,khd->hqk", query_heads, key_all, preferred_element_type=jnp.float32
    ) * (1.0 / math.sqrt(HEAD_DIM))
    scores = jnp.where(visible[None], scores, masked_score)
    top_score = jnp.max(scores, axis=2, keepdims=True)
    expo = jnp.exp(scores - top_score)
    weights_soft = (expo / jnp.sum(expo, axis=2, keepdims=True)).astype(jnp.bfloat16)
    attended = jnp.einsum(
        "hqk,khd->qhd", weights_soft, value_all, preferred_element_type=jnp.float32
    ).reshape(tok_rows, feat_width)
    stream = (residual_in.astype(jnp.float32) + attended).astype(jnp.bfloat16)
    send_width = stream.shape[1]
    blocks_dev = tok_rows // BLOCK
    piece_rows = BLOCK // seq_count
    spread_in = stream.reshape(blocks_dev, seq_count, piece_rows, send_width)
    spread_out = lax.all_to_all(spread_in, "seq", split_axis=1, concat_axis=0, tiled=True)
    block_count = blocks_dev * seq_count
    spread_rows = spread_out.reshape(block_count, piece_rows, send_width)
    expert_ids = routing[:, 0]
    expert_count = seq_count // 2
    most_blocks = min(2 * block_count // expert_count, block_count - expert_count + 1)
    order_index = jnp.arange(block_count, dtype=jnp.int32)
    same_expert = expert_ids[None, :] == expert_ids[:, None]
    rank_of = jnp.sum(same_expert & (order_index[None, :] < order_index[:, None]), axis=1)
    expert_range = jnp.arange(expert_count, dtype=jnp.int32)
    slot_range = jnp.arange(most_blocks, dtype=jnp.int32)
    selector = (
        (expert_ids[None, None, :] == expert_range[:, None, None])
        & (rank_of[None, None, :] == slot_range[None, :, None])
    ).astype(jnp.bfloat16)
    picked = jnp.einsum(
        "erb,bqf->erqf", selector, spread_rows, preferred_element_type=jnp.float32
    ).astype(jnp.bfloat16)
    outgoing = jnp.broadcast_to(
        picked[:, None], (expert_count, 2, most_blocks, piece_rows, send_width)
    )
    outgoing = outgoing.reshape(seq_count, most_blocks, piece_rows, send_width)
    features_full = lax.all_gather(
        lax.all_to_all(outgoing, "seq", split_axis=0, concat_axis=0, tiled=True),
        "tp",
        axis=3,
        tiled=True,
    )
    source_count = features_full.shape[0]
    slot_count = features_full.shape[1]
    stream_f32 = features_full.astype(jnp.float32)
    mean_square = jnp.mean(stream_f32 * stream_f32, axis=3, keepdims=True)
    normed = (stream_f32 * lax.rsqrt(mean_square + epsilon) * norm_gain).astype(jnp.bfloat16)
    normed = normed.reshape(-1, normed.shape[3])
    gate_val = jnp.dot(normed, gate_weight[0], preferred_element_type=jnp.float32)
    up_val = jnp.dot(normed, up_weight[0], preferred_element_type=jnp.float32)
    hidden = (jax.nn.silu(gate_val) * up_val).astype(jnp.bfloat16)
    hidden_half = lax.all_gather(hidden, "tp", axis=1, tiled=True)
    partial_value = jnp.dot(hidden_half, down_weight[0], preferred_element_type=jnp.float32).astype(
        jnp.bfloat16
    )
    partial_value = partial_value.reshape(source_count, slot_count, piece_rows, feat_width)
    returned = lax.all_to_all(partial_value, "seq", split_axis=0, concat_axis=0, tiled=True)
    returned = returned.reshape(expert_count, 2, most_blocks, piece_rows * feat_width)
    combined = jnp.einsum("erb,epry->pby", selector, returned, preferred_element_type=jnp.float32)
    residual_rows = spread_rows
    residual_rows = residual_rows.reshape(block_count, piece_rows * feat_width).astype(jnp.float32)
    finished = (residual_rows + combined[0] + combined[1]).astype(jnp.bfloat16)
    finished = finished.reshape(seq_count, blocks_dev, piece_rows, feat_width)
    restored = lax.all_to_all(finished, "seq", split_axis=0, concat_axis=2, tiled=True)
    return restored.reshape(tok_rows, feat_width)


BF16 = jnp.bfloat16
F32 = jnp.float32


def remote(src, dst, send_sem, recv_sem, device):
    return pltpu.make_async_remote_copy(
        src_ref=src,
        dst_ref=dst,
        send_sem=send_sem,
        recv_sem=recv_sem,
        device_id=device,
        device_id_type=pl.DeviceIdType.MESH,
    )


def layer_kernel(planes, most, arguments, out_ref, scratch):
    (
        routing_ref, q_ref, k_ref, v_ref, r_ref, gain_ref, gate_ref, up_ref, down_ref
    ) = arguments
    (
        q_buf,
        r_buf,
        kv_buf,
        line,
        end_out,
        end_in,
        x_buf,
        w_buf,
        acc_buf,
        square_buf,
        hid_buf,
        down_buf,
        mix,
        end_up,
        end_dn,
        up_out,
        up_in,
        dn_out,
        dn_in,
        fin_buf,
        pair_s,
        pair_r,
        local_s,
        kvline_s,
        kvline_r,
        line_s,
        line_r,
        end_s,
        end_r,
        feat_s,
        feat_r,
        hid_s,
        hid_r,
        ret_s,
        ret_r,
        edge_s,
        edge_r,
        last_s,
        last_r,
    ) = scratch
    rows = q_ref.shape[0]
    half = q_ref.shape[1] // 2
    heads = half // HEAD_DIM
    blocks = 2 * planes
    me = lax.axis_index("seq")
    t = lax.axis_index("tp")
    z = me // 2
    y = me % 2
    yo = 1 - y
    mate = 2 * z + yo
    tc = t + 1 - 2 * (t % 2)
    tx = t + 2 - 4 * (t // 2)
    txc = tx + 1 - 2 * (tx % 2)
    dev_y, dev_c, dev_x = (mate, t), (me, tc), (me, tx)
    dev_up, dev_dn = (me + 2, t), (me - 2, t)
    has_up, has_dn = z < planes - 1, z > 0
    unsent = []

    barrier = pltpu.get_barrier_semaphore()

    def greet(device):
        pl.semaphore_signal(
            barrier, inc=1, device_id=device, device_id_type=pl.DeviceIdType.MESH
        )

    for device in (dev_y, dev_c, dev_x):
        greet(device)
    pl.when(has_up)(lambda: greet(dev_up))
    pl.when(has_dn)(lambda: greet(dev_dn))

    def cols(which, h):
        return pl.ds(pl.multiple_of(which * half + h * HEAD_DIM, HEAD_DIM), HEAD_DIM)

    def wide(which):
        return pl.ds(pl.multiple_of(which * half, half), half)

    stay = []
    for h in range(heads):
        stay.append((k_ref.at[:, cols(y, h)], kv_buf.at[0, h, 0, y]))
        stay.append((v_ref.at[:, cols(y, h)], kv_buf.at[0, h, 1, y]))
    stay.append((q_ref.at[:, wide(y)], q_buf.at[y]))
    stay.append((r_ref.at[:, wide(y)], r_buf.at[y]))
    stay.append((gate_ref.at[0], w_buf.at[:, pl.ds(0, gate_ref.shape[2])]))
    stay.append((up_ref.at[0], w_buf.at[:, pl.ds(gate_ref.shape[2], gate_ref.shape[2])]))
    stay.append((down_ref.at[0, :, wide(y)], down_buf.at[y]))
    stay = [pltpu.make_async_copy(a, b, local_s.at[i]) for i, (a, b) in enumerate(stay)]
    for copy in stay:
        copy.start()

    expert = [routing_ref[b] for b in range(blocks)]
    slot = []
    for b in range(blocks):
        count = jnp.int32(0)
        for j in range(b):
            count = count + jnp.where(expert[j] == expert[b], 1, 0)
        slot.append(jnp.minimum(count, most - 1))

    def listing(which):
        found = []
        for r in range(most):
            index = jnp.int32(0)
            for b in range(blocks):
                index = jnp.where((expert[b] == which) & (slot[b] == r), b, index)
            found.append(index)
        return found

    chosen = listing(z)
    at_edge = (z == 0) | (z == planes - 1)
    by_edge = (z == 1) | (z == planes - 2)
    chosen_edge = listing(jnp.where(z == 1, 0, planes - 1))
    dev_edge = (jnp.where(z == 1, me - 2, me + 2), t)
    line_up, line_dn = z < planes - 2, z > 1

    for dist in (1, 2):

        @pl.when(z < dist)
        def _():
            kv_buf[dist] = jnp.zeros(kv_buf.shape[1:], kv_buf.dtype)

    pl.semaphore_wait(
        barrier, 3 + jnp.where(has_up, 1, 0) + jnp.where(has_dn, 1, 0)
    )

    def pair_copy(i, src, dst):
        return remote(src, dst, pair_s.at[i], pair_r.at[i], dev_y)

    swap, landed = [], []
    for h in range(heads):
        for n, ref in enumerate((k_ref, v_ref)):
            i = len(swap)
            swap.append(pair_copy(i, ref.at[:, cols(yo, h)], kv_buf.at[0, h, n, y]))
            landed.append(pair_copy(i, kv_buf.at[0, h, n, yo], kv_buf.at[0, h, n, yo]))
    for ref, buf in ((q_ref, q_buf), (r_ref, r_buf)):
        i = len(swap)
        swap.append(pair_copy(i, ref.at[:, wide(yo)], buf.at[y]))
        landed.append(pair_copy(i, buf.at[yo], buf.at[yo]))
    i = len(swap)
    swap.append(pair_copy(i, down_ref.at[0, :, wide(yo)], down_buf.at[y + 2]))
    landed.append(pair_copy(i, down_buf.at[yo + 2], down_buf.at[yo + 2]))
    for copy in swap:
        copy.start()
        unsent.append((None, copy))

    def kv_copy(dist, h):
        return remote(
            kv_buf.at[dist, h],
            kv_buf.at[dist + 1, h],
            kvline_s.at[dist, h],
            kvline_r.at[dist, h],
            dev_up,
        )

    def kv_own(h):
        for i in (2 * h, 2 * h + 1):
            stay[i].wait()
            landed[i].wait_recv()
        pl.when(has_up)(lambda: kv_copy(0, h).start())
        unsent.append((has_up, kv_copy(0, h)))

    def kv_relay(h):
        pl.when(has_dn)(lambda: kv_copy(0, h).wait_recv())
        pl.when(has_dn & has_up)(lambda: kv_copy(1, h).start())
        unsent.append((has_dn & has_up, kv_copy(1, h)))

    def line_copy(way, plane, h):
        return remote(
            line[h].at[plane],
            line[h].at[plane],
            line_s.at[way, plane, h],
            line_r.at[way, plane, h],
            dev_up if way == 0 else dev_dn,
        )

    row_at = lax.broadcasted_iota(jnp.int32, (rows, rows), 0)
    col_at = lax.broadcasted_iota(jnp.int32, (rows, rows), 1)
    behind = [jnp.where(z >= dist, 0.0, masked_score).astype(F32) for dist in range(3)]

    def attend(h):
        pl.when(z > 1)(lambda: kv_copy(1, h).wait_recv())
        at = pl.ds(h * HEAD_DIM, HEAD_DIM)
        count = WINDOW // rows
        for n in range(2):
            query = q_buf[n, :, at]
            places = []
            for back in range(count + 1):
                dist = (back - n + 1) // 2
                places.append((dist, (n - back) % 2))
            parts = []
            for back, (dist, block) in enumerate(places):
                part = lax.dot_general(
                    query,
                    kv_buf[dist, h, 0, block],
                    (((1,), (1,)), ((), ())),
                    preferred_element_type=F32,
                )
                if back == 0:
                    part = jnp.where(col_at <= row_at, part, masked_score)
                if back == count:
                    part = jnp.where(col_at > row_at, part, masked_score)
                if dist > 0:
                    part = part + behind[dist]
                parts.append(part)
            top = parts[0]
            for part in parts[1:]:
                top = jnp.maximum(top, part)
            top = jnp.max(top, axis=1, keepdims=True)
            parts = [jnp.exp((part - top) * (1.0 / math.sqrt(HEAD_DIM))) for part in parts]
            total = parts[0]
            for part in parts[1:]:
                total = total + part
            share = 1.0 / jnp.sum(total, axis=1, keepdims=True)
            attended = jnp.dot(
                jnp.concatenate([(part * share).astype(BF16) for part in parts], axis=1),
                jnp.concatenate([kv_buf[dist, h, 1, block] for dist, block in places], axis=0),
                preferred_element_type=F32,
            )
            line[h][z, n] = (r_buf[n, :, at].astype(F32) + attended).astype(BF16)
        pl.when(line_up)(lambda: line_copy(0, z, h).start())
        pl.when(line_dn)(lambda: line_copy(1, z, h).start())
        unsent.append((line_up, line_copy(0, z, h)))
        unsent.append((line_dn, line_copy(1, z, h)))

    def end_copy(h):
        return remote(end_out[h], end_in[h], end_s.at[h], end_r.at[h], dev_edge)

    def pick(flag, a, b):
        mask = jnp.full(a.shape, flag.astype(jnp.int32), jnp.int32) > 0
        return jnp.where(mask, a.astype(F32), b.astype(F32)).astype(BF16)

    def spread(h):
        for step in range(1, planes):
            below, above = z - step, z + step
            from_below = (below >= 0) & (z < planes - 1)
            from_above = (above < planes) & (z > 0)

            @pl.when(from_below)
            def _():
                line_copy(0, below, h).wait_recv()
                pl.when(line_up)(lambda: line_copy(0, below, h).start())

            @pl.when(from_above)
            def _():
                line_copy(1, above, h).wait_recv()
                pl.when(line_dn)(lambda: line_copy(1, above, h).start())

            unsent.append((from_below & line_up, line_copy(0, below, h)))
            unsent.append((from_above & line_dn, line_copy(1, above, h)))

        @pl.when(by_edge)
        def _():
            for r in range(most):
                end_out[h][r] = line[h][chosen_edge[r] // 2, chosen_edge[r] % 2]
            end_copy(h).start()

        unsent.append((by_edge, end_copy(h)))

        @pl.when(at_edge)
        def _():
            end_copy(h).wait_recv()
            for r in range(most):
                x_buf[y, t, h, pl.ds(r * rows, rows)] = pick(
                    chosen[r] // 2 == z, line[h][z, chosen[r] % 2], end_in[h][r]
                )

        @pl.when(jnp.logical_not(at_edge))
        def _():
            for r in range(most):
                x_buf[y, t, h, pl.ds(r * rows, rows)] = line[h][chosen[r] // 2, chosen[r] % 2]

    def gatherer(buf, sends, recvs, h):
        middle = buf.shape[3] // 2
        low, high, whole = pl.ds(0, middle), pl.ds(middle, middle), pl.ds(0, 2 * middle)

        def piece(i, at, device):
            ref = buf.at[at[0], at[1], h, at[2]]
            return remote(ref, ref, sends.at[i, h], recvs.at[i, h], device)

        def send(i, at, device):
            piece(i, at, device).start()
            unsent.append((None, piece(i, at, device)))

        def take(i, at):
            piece(i, at, dev_c).wait_recv()

        def first():
            send(0, (y, t, low), dev_x)
            send(1, (y, t, high), dev_y)
            send(2, (y, t, high), dev_x)
            send(3, (y, t, low), dev_y)
            send(4, (y, t, whole), dev_c)

        def second():
            take(0, (y, tx, low))
            send(5, (y, tx, low), dev_y)
            send(7, (y, tx, low), dev_c)
            take(1, (yo, t, high))
            send(6, (yo, t, high), dev_x)
            send(8, (yo, t, high), dev_c)
            take(2, (y, tx, high))
            send(9, (y, tx, high), dev_c)
            take(3, (yo, t, low))
            send(10, (yo, t, low), dev_c)

        def third():
            take(5, (yo, tx, low))
            send(11, (yo, tx, low), dev_c)
            take(6, (yo, tx, high))
            send(12, (yo, tx, high), dev_c)

        def near():
            take(4, (y, tc, whole))
            take(7, (y, txc, low))
            take(9, (y, txc, high))
            take(8, (yo, tc, high))
            take(10, (yo, tc, low))

        def far():
            take(11, (yo, txc, low))
            take(12, (yo, txc, high))

        return first, second, third, near, far

    def expert_parts(parts, pair):
        left, right = [], []
        square = square_buf[...]
        for py, pt in parts:
            for h in (2 * pair, 2 * pair + 1):
                start = pl.multiple_of((2 * pt + py) * half + h * HEAD_DIM, HEAD_DIM)
                x = x_buf[py, pt, h].astype(F32)
                square = square + jnp.sum(x * x, axis=1, keepdims=True)
                left.append((x * gain_ref[:, pl.ds(start, HEAD_DIM)]).astype(BF16))
                right.append(w_buf[pl.ds(start, HEAD_DIM), :])
        square_buf[...] = square
        acc_buf[...] += jnp.dot(
            jnp.concatenate(left, axis=1),
            jnp.concatenate(right, axis=0),
            preferred_element_type=F32,
        )

    stages = [gatherer(x_buf, feat_s, feat_r, h) for h in range(heads)]
    most_parts = [(y, t), (y, tc), (y, tx), (yo, t), (y, txc), (yo, tc)]
    rest_parts = [(yo, tx), (yo, txc)]
    for h in range(heads):
        kv_own(h)
    kv_relay(0)
    for i in (2 * heads, 2 * heads + 1):
        stay[i].wait()
        landed[i].wait_recv()
    for turn in range(heads + 3):
        if turn + 1 < heads:
            kv_relay(turn + 1)
        if turn < heads:
            attend(turn)
        if turn == heads:
            acc_buf[...] = jnp.zeros_like(acc_buf)
            square_buf[...] = jnp.zeros_like(square_buf)
            for copy in stay[2 * heads + 2 :]:
                copy.wait()
        if 0 <= turn - 1 < heads:
            spread(turn - 1)
            stages[turn - 1][0]()
        if 0 <= turn - 2 < heads:
            stages[turn - 2][1]()
        if 0 <= turn - 3 < heads:
            h = turn - 3
            if h == heads - 1:
                stages[h][3]()
                expert_parts(most_parts, h // 2)
            stages[h][2]()
            if h < heads - 1:
                stages[h][3]()
            stages[h][4]()
            if h == heads - 1:
                expert_parts(rest_parts, h // 2)
            elif h % 2 == 1:
                expert_parts(most_parts + rest_parts, h // 2)
    units = gate_ref.shape[2]
    features = gain_ref.shape[1]
    scale = lax.rsqrt(square_buf[...] * (1.0 / features) + epsilon)
    gate_val = acc_buf[:, pl.ds(0, units)] * scale
    up_val = acc_buf[:, pl.ds(units, units)] * scale
    hid_buf[y, t, 0] = (gate_val / (1.0 + jnp.exp(-gate_val)) * up_val).astype(BF16)
    for stage in gatherer(hid_buf, hid_s, hid_r, 0):
        stage()

    chunks = len(mix)
    span = half // chunks
    per = span // HEAD_DIM

    def edge_copy(way, c):
        dst = end_up[c] if way == 0 else end_dn[c]
        return remote(
            mix[c], dst, edge_s.at[way, c], edge_r.at[way, c], dev_up if way == 0 else dev_dn
        )

    def ret_copy(way, d, c):
        out, arrived = (up_out, up_in) if way == 0 else (dn_out, dn_in)
        return remote(
            out.at[c, d],
            arrived.at[c, d],
            ret_s.at[way, d, c],
            ret_r.at[way, d, c],
            dev_up if way == 0 else dev_dn,
        )

    landed[2 * heads + 2].wait_recv()
    hidden = [
        jnp.concatenate([hid_buf[h, i, 0] for i in range(hid_buf.shape[1])], axis=1)
        for h in range(2)
    ]
    for c in range(chunks):
        total = jnp.concatenate(
            [x_buf[y, t, c * per + i] for i in range(per)], axis=1
        ).astype(F32)
        for h in range(2):
            weight = down_buf[h + 2 * ((y + h) % 2), :, pl.ds(c * span, span)]
            branch = jnp.dot(hidden[h], weight, preferred_element_type=F32).astype(BF16)
            total = total + branch.astype(F32)
        mix[c][...] = total.astype(BF16).reshape(most, rows, span)
        pl.when(z == 0)(lambda: edge_copy(0, c).start())
        pl.when(z == planes - 1)(lambda: edge_copy(1, c).start())
        unsent.append((z == 0, edge_copy(0, c)))
        unsent.append((z == planes - 1, edge_copy(1, c)))

    def relay(c, close):
        if close:
            pl.when(z == 1)(lambda: edge_copy(0, c).wait_recv())
            pl.when(z == planes - 2)(lambda: edge_copy(1, c).wait_recv())
        for step in range(planes - 1):
            for way, d in ((0, planes - 1 - step), (1, step)):
                passes = (z < d) & (z > 0) if way == 0 else (z > d) & (z < planes - 1)
                near = z == 1 if way == 0 else z == planes - 2
                end = end_up[c] if way == 0 else end_dn[c]
                out, arrived = (up_out, up_in) if way == 0 else (dn_out, dn_in)
                here = passes & near if close else passes & jnp.logical_not(near)

                @pl.when(here)
                def _():
                    if not close:
                        ret_copy(way, d, c).wait_recv()
                    for n in range(2):
                        b = 2 * d + n
                        other = end[slot[b]] if close else arrived[c, d, n]
                        out[c, d, n] = pick(expert[b] == z, mix[c][slot[b]], other)
                    ret_copy(way, d, c).start()

                unsent.append((here, ret_copy(way, d, c)))

    def finish(which, c):
        return pl.ds(pl.multiple_of(which * half + c * span, span), span)

    def last_copy(c):
        return remote(
            fin_buf.at[c, yo], out_ref.at[:, finish(y, c)], last_s.at[c], last_r.at[c], dev_y
        )

    def arrive(c):
        for d in range(planes):

            @pl.when(z == d)
            def _():
                if d > 1:
                    ret_copy(0, d, c).wait_recv()
                if d < planes - 2:
                    ret_copy(1, d, c).wait_recv()
                for n in range(2):
                    b = 2 * d + n
                    value = mix[c][slot[b]]
                    if d > 0:
                        value = pick(
                            expert[b] < z, up_in[c, d, n] if d > 1 else end_up[c][slot[b]], value
                        )
                    if d < planes - 1:
                        value = pick(
                            expert[b] > z,
                            dn_in[c, d, n] if d < planes - 2 else end_dn[c][slot[b]],
                            value,
                        )
                    fin_buf[c, n] = value

        last_copy(c).start()
        unsent.append((None, last_copy(c)))
        out_ref[:, finish(y, c)] = fin_buf[c, y]
    relay(0, True)
    for c in range(chunks):
        if c + 1 < chunks:
            relay(c + 1, True)
        relay(c, False)
        if c > 0:
            arrive(c - 1)
    arrive(chunks - 1)
    for c in range(chunks):
        mine = out_ref.at[:, finish(yo, c)]
        remote(mine, mine, last_s.at[c], last_r.at[c], dev_y).wait_recv()
    for flag, copy in unsent:
        if flag is None:
            copy.wait_send()
        else:
            pl.when(flag)(lambda: copy.wait_send())


def local(
    queries, keys, values, residual_in, norm_gain, routing, gate_weight, up_weight, down_weight
):
    seq_count = lax.axis_size("seq")
    tp_count = lax.axis_size("tp")
    rows, width = queries.shape
    units = gate_weight.shape[2]
    planes = seq_count // 2
    fits = (
        tp_count == 4
        and seq_count % 2 == 0
        and 4 <= planes <= 8
        and rows == BLOCK
        and WINDOW == 4 * rows
        and units == 128
        and width % (8 * HEAD_DIM) == 0
    )
    if not fits:
        return local_general(
            queries,
            keys,
            values,
            residual_in,
            norm_gain,
            routing,
            gate_weight,
            up_weight,
            down_weight,
        )
    half = width // 2
    heads = half // HEAD_DIM
    most = min(2 * seq_count // planes, seq_count - planes + 1)
    chunks = 4
    span = half // chunks
    vmem = pl.BlockSpec(memory_space=pltpu.VMEM)
    anywhere = pl.BlockSpec(memory_space=pltpu.MemorySpace.HBM)
    dma = pltpu.SemaphoreType.DMA

    def room(*shape, kind=BF16):
        return pltpu.VMEM(shape, kind)

    scratch = (
        room(2, rows, half),
        room(2, rows, half),
        room(3, heads, 2, 2, rows, HEAD_DIM),
        [room(planes, 2, rows, HEAD_DIM) for _ in range(heads)],
        [room(most, rows, HEAD_DIM) for _ in range(heads)],
        [room(most, rows, HEAD_DIM) for _ in range(heads)],
        room(2, tp_count, heads, most * rows, HEAD_DIM),
        room(norm_gain.shape[0], 2 * units),
        room(most * rows, 2 * units, kind=F32),
        room(most * rows, 1, kind=F32),
        room(2, tp_count, 1, most * rows, units),
        room(4, down_weight.shape[1], half),
        [room(most, rows, span) for _ in range(chunks)],
        [room(most, rows, span) for _ in range(chunks)],
        [room(most, rows, span) for _ in range(chunks)],
        room(chunks, planes, 2, rows, span),
        room(chunks, planes, 2, rows, span),
        room(chunks, planes, 2, rows, span),
        room(chunks, planes, 2, rows, span),
        room(chunks, 2, rows, span),
        dma((2 * heads + 3,)),
        dma((2 * heads + 3,)),
        dma((2 * heads + 5,)),
        dma((2, heads)),
        dma((2, heads)),
        dma((2, planes, heads)),
        dma((2, planes, heads)),
        dma((heads,)),
        dma((heads,)),
        dma((13, heads)),
        dma((13, heads)),
        dma((13, 1)),
        dma((13, 1)),
        dma((2, planes, chunks)),
        dma((2, planes, chunks)),
        dma((2, chunks)),
        dma((2, chunks)),
        dma((chunks,)),
        dma((chunks,)),
    )
    flat, tree = jax.tree.flatten(scratch, is_leaf=lambda leaf: not isinstance(leaf, (list, tuple)))

    def kernel(*refs):
        layer_kernel(planes, most, refs[:9], refs[9], jax.tree.unflatten(tree, refs[10:]))

    return pl.pallas_call(
        kernel,
        name="layer",
        out_shape=jax.ShapeDtypeStruct((rows, width), BF16),
        in_specs=[pl.BlockSpec(memory_space=pltpu.SMEM)]
        + [anywhere] * 4
        + [vmem]
        + [anywhere] * 3,
        out_specs=vmem,
        scratch_shapes=flat,
        compiler_params=pltpu.CompilerParams(
            collective_id=0, has_side_effects=True, vmem_limit_bytes=67043328
        ),
    )(
        routing.reshape(-1),
        queries,
        keys,
        values,
        residual_in,
        norm_gain.reshape(1, -1),
        gate_weight,
        up_weight,
        down_weight,
    )


def solution(mesh):
    in_specs = (
        P("seq", "tp"),
        P("seq", "tp"),
        P("seq", "tp"),
        P("seq", "tp"),
        P(),
        P(),
        P("seq", None, "tp"),
        P("seq", None, "tp"),
        P("seq", None, "tp"),
    )
    out_specs = P("seq", "tp")
    return jax.shard_map(local, mesh=mesh, in_specs=in_specs, out_specs=out_specs, check_vma=False)
```
